32 devices in a mesh: seq: 4 (over y, x), feat: 8 (over z, core).
Axes of the slice: x: 2, y: 2, z: 4, core: 2. Of those that a mesh axis runs over, the one named last changes fastest.
Arguments:
- activations: bfloat16 [512, 4096], P('seq', 'feat'), may hold values from -40 to 40
- query_weight: bfloat16 [4096, 4096], P('feat'), may hold values from -0.140625 to 0.140625
- key_weight: bfloat16 [4096, 1024], P('feat'), may hold values from -0.09375 to 0.09375
- value_weight: bfloat16 [4096, 1024], P('feat'), may hold values from -0.09375 to 0.09375
- document_ids: int32 [512], replicated, may hold values from 0 to 5, never falling along the last dimension, each value on 1 to 256 neighbouring positions
Outputs:
- attended: bfloat16 [512, 4096], P('seq', 'feat')
The draws below stay inside these ranges and needn't reach their ends.
Inputs may be any that keep to these rules, and one draw needn't show every extreme that they name: `document_ids`: document ids by sequence position, never falling.
All inputs are finite; a program needn't handle non-finite values.
Results may differ from the reference program's by a relative error of at most 0.02.
Values may be sent and summed in bfloat16 or wider, within the bound.
A program may use at most 64 MiB of HBM per device.

```python
import math
import jax
import jax.numpy as jnp
import numpy as np
from jax import lax

D = 4096
H = 32
KVH = 8
HD = 128
TOK_DEV = 128
DOCS = 6
TOKENS = 512
DOC_MOST = 256
N_SEQ = 4
N_FEAT = 8


def draw_activations(key, part):
    base_rows = jnp.clip(jax.random.normal(jax.random.fold_in(key, 1), (TOKENS, D), jnp.float32), -6.0, 6.0)
    result = base_rows
    return result.astype(jnp.bfloat16)


def weight_pair(key):
    key_part = jnp.clip(jax.random.normal(jax.random.fold_in(key, 11), (D, KVH * HD), jnp.float32), -6.0, 6.0) * D ** (-0.5)
    query_part = jnp.clip(jax.random.normal(jax.random.fold_in(key, 12), (D, H * HD), jnp.float32), -6.0, 6.0) * D ** (-0.5)
    return (query_part, key_part)


def draw_query_weight(key, part):
    return weight_pair(key)[0].astype(jnp.bfloat16)


def draw_key_weight(key, part):
    return weight_pair(key)[1].astype(jnp.bfloat16)


def levels(rng, shape, cuts, least, high):
    def one(axis_at, parts):
        draws = jax.random.uniform(jax.random.fold_in(jax.random.fold_in(rng, 6), axis_at), (parts,), jnp.float32, least / len(cuts), high / len(cuts))
        return jnp.repeat(jnp.exp(draws), shape[axis_at] // parts).reshape((-1,) + (1,) * (len(shape) - axis_at - 1))

    gain = one(*cuts[0])
    for cut in cuts[1:]:
        gain = gain * one(*cut)
    return gain


def length_profile(amount, total, bound, slope):
    weights = [(1 << 20) // math.isqrt(rank ** slope) + 1 for rank in range(2, amount + 1)]
    spare, holding = total - bound - (amount - 1), [1] * (amount - 1)
    while spare > 0:
        movable = [i for i in range(amount - 1) if holding[i] < bound]
        whole, remaining = sum([weights[i] for i in movable]), spare
        for i in movable:
            addition = min(bound - holding[i], max(1, remaining * weights[i] // whole), spare)
            holding[i] = holding[i] + addition
            spare = spare - addition
    return np.array([bound] + holding)


def ragged(own_key, amount, total, reach, lean):
    if amount == 2:
        one = jax.random.randint(own_key, (), max(1, total - reach), min(reach, total - 1) + 1)
        return jnp.stack([one, total - one])
    tallies = jnp.asarray(length_profile(amount, total, reach, lean), jnp.int32)
    twos = (amount - 1) // 2
    source_of, receiver = tallies[1:1 + 2 * twos:2], tallies[2:2 + 2 * twos:2]
    room = jnp.minimum(source_of - 1, reach - receiver)
    moved = jax.random.randint(jax.random.fold_in(own_key, 1), (twos,), 0, 1 << 20) % (room + 1)
    tallies = tallies.at[1:1 + 2 * twos:2].set(source_of - moved).at[2:2 + 2 * twos:2].set(receiver + moved)
    return tallies[jax.random.permutation(jax.random.fold_in(own_key, 2), amount)]


def bell_draw(key, extent, spread, reach, cuts=(), kind=jnp.bfloat16):
    values = spread * jax.random.normal(key, extent, jnp.float32)
    if cuts:
        values = values * levels(key, extent, cuts, -0.22, 0.18)
    return jnp.clip(values, -reach, reach).astype(kind)


def setup_inputs(seed: int = 0) -> dict:
    arg_keys = jax.random.split(jax.random.key(seed), 6)
    return {
        "activations": draw_activations(jax.random.fold_in(arg_keys[5], 71), 0),
        "query_weight": draw_query_weight(jax.random.fold_in(arg_keys[5], 71), 0),
        "key_weight": draw_key_weight(jax.random.fold_in(arg_keys[5], 71), 0),
        "value_weight": bell_draw(arg_keys[3], (D, KVH * HD), D ** -0.5, 0.09375, ((0, 8),)),
        "document_ids": jnp.searchsorted(jnp.cumsum(ragged(arg_keys[4], DOCS, TOKENS, DOC_MOST, 2)), jnp.arange(TOKENS), side="right").astype(jnp.int32),
    }


def project(activations, weight):
    local_width = D // N_FEAT
    columns = weight.shape[1]
    pieces = activations.reshape(TOKENS, N_FEAT, local_width).transpose(1, 0, 2)
    blocks = weight.reshape(N_FEAT, local_width, columns)

    def accumulate(running_sum, inputs):
        part_rows, part_weight = inputs
        partial_sum = jnp.dot(part_rows, part_weight, preferred_element_type=jnp.float32).astype(jnp.bfloat16)
        partial_sum = lax.optimization_barrier(partial_sum)
        return running_sum + partial_sum.astype(jnp.float32), None

    running_sum, unused = lax.scan(accumulate, jnp.zeros((TOKENS, columns), jnp.float32), (pieces, blocks))
    return running_sum.astype(jnp.bfloat16)


def reference(activations, query_weight, key_weight, value_weight, document_ids):
    queries = project(activations, query_weight).reshape(TOKENS, H, HD).transpose(1, 0, 2)
    keys_all = project(activations, key_weight).reshape(TOKENS, KVH, HD).transpose(1, 0, 2)
    values_all = project(activations, value_weight).reshape(TOKENS, KVH, HD).transpose(1, 0, 2)
    rowidx = jnp.arange(TOKENS, dtype=jnp.int32)
    positions = (rowidx % TOK_DEV) * N_SEQ + rowidx // TOK_DEV
    documents = document_ids[positions]
    allowed = (positions[None, :] <= positions[:, None]) & (documents[None, :] == documents[:, None])
    group_size = H // KVH
    score_scale = HD ** -0.5

    def one_head(head_index):
        query_rows = queries[head_index]
        key_rows = keys_all[head_index // group_size]
        value_rows = values_all[head_index // group_size]
        scores = jnp.dot(query_rows, key_rows.T, preferred_element_type=jnp.float32) * score_scale
        masked = jnp.where(allowed, scores, -1e30)
        largest = jnp.max(masked, axis=1, keepdims=True)
        weights = jnp.where(allowed, jnp.exp(scores - largest), 0.0)
        totals = jnp.sum(weights, axis=1, keepdims=True)
        weighted = jnp.dot(weights.astype(jnp.bfloat16), value_rows, preferred_element_type=jnp.float32)
        return (weighted / totals).astype(jnp.bfloat16)

    heads_out = lax.map(one_head, jnp.arange(H, dtype=jnp.int32))
    return heads_out.transpose(1, 0, 2).reshape(TOKENS, H * HD)
```

```python
import jax
import jax.numpy as jnp
from jax import lax
from jax.experimental import pallas as pl
from jax.experimental.pallas import tpu as pltpu
from jax.sharding import PartitionSpec as P

H = 32
KVH = 8
HD = 128


def passed_along(value, axis, steps):
    count = lax.axis_size(axis)
    pairs = [(source, (source + steps) % count) for source in range(count)]
    return lax.ppermute(value, axis, pairs)


def attend_block(
    softmax_state, kv_block, source, query_heads, query_pos, query_doc, doc_table, stripes
):
    maxima, totals, accumulated = softmax_state
    row_count = kv_block.shape[0]
    head_size = kv_block.shape[1] // 2
    key_rows = kv_block[:, :head_size]
    value_rows = kv_block[:, head_size:]
    key_pos = jnp.arange(row_count, dtype=jnp.int32) * stripes + source
    key_doc = lax.dynamic_slice_in_dim(doc_table, source, 1, 1)[:, 0]
    allowed = (key_pos[None, :] <= query_pos[:, None]) & (key_doc[None, :] == query_doc[:, None])
    scores = jnp.einsum(
        "qhd,kd->hqk", query_heads, key_rows, preferred_element_type=jnp.float32
    ) * head_size ** (-0.5)
    masked = jnp.where(allowed[None], scores, -1e30)
    newmax = jnp.maximum(maxima, jnp.max(masked, axis=2))
    weights = jnp.where(allowed[None], jnp.exp(scores - newmax[..., None]), 0.0)
    factor = jnp.exp(maxima - newmax)
    totals = totals * factor + jnp.sum(weights, axis=2)
    accumulated = accumulated * factor[..., None] + jnp.einsum(
        "hqk,kd->hqd", weights.astype(jnp.bfloat16), value_rows, preferred_element_type=jnp.float32
    )
    return (newmax, totals, accumulated)


def local(activations, query_weight, key_weight, value_weight, document_ids):
    row_count = activations.shape[0]
    features = lax.axis_size("feat")
    stripes = lax.axis_size("seq")
    seq_rank = lax.axis_index("seq")
    per_device = H // features
    group_size = H // KVH
    query_part = jnp.dot(activations, query_weight, preferred_element_type=jnp.float32).astype(
        jnp.bfloat16
    )
    key_part = jnp.dot(activations, key_weight, preferred_element_type=jnp.float32).astype(
        jnp.bfloat16
    )
    value_part = jnp.dot(activations, value_weight, preferred_element_type=jnp.float32).astype(
        jnp.bfloat16
    )
    owners = [rank * per_device // group_size for rank in range(features)]

    def by_owner(part):
        return jnp.stack([part[:, owner * HD : (owner + 1) * HD] for owner in owners], axis=1)

    stacked = jnp.concatenate(
        [
            query_part.reshape(row_count, features, per_device * HD),
            by_owner(key_part),
            by_owner(value_part),
        ],
        axis=2,
    ).reshape(row_count, features * (per_device + 2) * HD)
    summed = (
        lax.psum_scatter(stacked, "feat", scatter_dimension=1, tiled=True)
        .astype(jnp.float32)
        .astype(jnp.bfloat16)
    )
    queries = summed[:, : per_device * HD]
    kv_block = summed[:, per_device * HD :]
    query_heads = queries.reshape(row_count, per_device, HD)
    query_pos = jnp.arange(row_count, dtype=jnp.int32) * stripes + seq_rank
    doc_table = document_ids.reshape(row_count, stripes)
    query_doc = lax.dynamic_slice_in_dim(doc_table, seq_rank, 1, 1)[:, 0]

    def visit_block(running, current, source):
        return attend_block(
            running, current, source, query_heads, query_pos, query_doc, doc_table, stripes
        )

    softmax_state = (
        jnp.full((per_device, row_count), -1e30, jnp.float32),
        jnp.zeros((per_device, row_count), jnp.float32),
        jnp.zeros((per_device, row_count, HD), jnp.float32),
    )
    softmax_state = visit_block(softmax_state, kv_block, seq_rank)

    def advance(cycle_step, loop_carry):
        current, running = loop_carry
        current = passed_along(current, "seq", 1)
        return (current, visit_block(running, current, (seq_rank - cycle_step) % stripes))

    loop_carry = lax.fori_loop(1, stripes, advance, (kv_block, softmax_state))
    softmax_state = loop_carry[1]
    maxima, totals, accumulated = softmax_state
    output = (accumulated / totals[..., None]).astype(jnp.bfloat16)
    return output.transpose(1, 0, 2).reshape(row_count, per_device * HD)


MESH = pl.DeviceIdType.MESH
ROWS = 128
HALF = 64
WIDE = 256
PIECES = 3
CHIPS = 4
STRIPES = 4
BF = jnp.bfloat16
F32 = jnp.float32


def fused_kernel(
    x_hbm, doc_hbm, wq_hbm, wk_hbm, wv_hbm, o_ref,
    x, doc, wq, wk, wv, part, sib, zin, kv, bias,
    in_sem, w_sem, sib_send, sib_recv, z_send, z_recv, kv_send, kv_recv,
):
    s = lax.axis_index("seq")
    f = lax.axis_index("feat")
    z = f // 2
    c = f % 2
    other = 1 - c
    sibling = (s, f + 1 - 2 * c)
    right = z // 2
    end = 3 * right
    is_end = z == end
    is_mid = z != end
    ends = is_end.astype(jnp.int32)
    near = z + 1 - 2 * (z % 2)
    far_end = 3 - end
    far_mid = 2 - right
    q_order = (far_end, far_mid, near, z)
    kv_order = (
        far_end + ends * (far_mid - far_end), far_mid + ends * (far_end - far_mid), near, z,
    )
    peers = (s + 1 - 2 * (s % 2), s + 2 - 4 * (s // 2), 3 - s)

    barrier = pltpu.get_barrier_semaphore()
    pl.semaphore_signal(barrier, inc=1, device_id=sibling, device_id_type=MESH)
    for dz in range(1, CHIPS):
        pl.semaphore_signal(
            barrier, inc=1, device_id=(s, 2 * ((z + dz) % CHIPS) + c), device_id_type=MESH
        )
    for peer in peers:
        pl.semaphore_signal(barrier, inc=1, device_id=(peer, f), device_id_type=MESH)

    def weight_copy(kind, k):
        source, held, width = ((wq_hbm, wq, 1024), (wk_hbm, wk, 256), (wv_hbm, wv, 256))[kind]
        order = kv_order if kind else q_order
        at = pl.multiple_of(order[k] * width, 128)
        return pltpu.make_async_copy(source.at[:, pl.ds(at, width)], held.at[k], w_sem.at[kind, k])

    x_copy = pltpu.make_async_copy(x_hbm, x, in_sem.at[0])
    doc_copy = pltpu.make_async_copy(doc_hbm, doc, in_sem.at[1])
    x_copy.start()
    for k in range(CHIPS):
        weight_copy(1, k).start()
        weight_copy(2, k).start()
    for k in range(CHIPS):
        weight_copy(0, k).start()
    doc_copy.start()

    def dot(a, b):
        return jnp.dot(a, b, preferred_element_type=F32)

    def sib_copy(p, k):
        return pltpu.make_async_remote_copy(
            src_ref=part.at[other, p, k], dst_ref=sib.at[p, k],
            send_sem=sib_send.at[p, k], recv_sem=sib_recv.at[p, k],
            device_id=sibling, device_id_type=MESH,
        )

    def project(p, k):
        rows = x[...]
        if p == 0:
            weight_copy(1, k).wait()
            weight_copy(2, k).wait()
            keys = dot(rows, wk[k]).astype(BF)
            values = dot(rows, wv[k]).astype(BF)
            for lane in range(2):
                part[lane, 0, k, :, :HD] = keys[:, lane * HD : (lane + 1) * HD]
                part[lane, 0, k, :, HD:] = values[:, lane * HD : (lane + 1) * HD]
        else:
            for lane in range(2):
                at = lane * 512 + (p - 1) * WIDE
                part[lane, p, k] = dot(rows, wq[k, :, at : at + WIDE]).astype(BF)

    def half(h):
        return slice(h * HALF, (h + 1) * HALF)

    def z_copy(p, k, h, chip, slot):
        return pltpu.make_async_remote_copy(
            src_ref=part.at[c, p, k, half(h)], dst_ref=zin.at[p, slot, half(h)],
            send_sem=z_send.at[p, k, h], recv_sem=z_recv.at[p, slot, h],
            device_id=(s, 2 * chip + c), device_id_type=MESH,
        )

    def z_arrival(p, slot, h):
        z_copy(p, 0, h, near, slot).wait_recv()

    def pair_sum(p, k):
        return part[c, p, k].astype(F32) + sib[p, k].astype(F32)

    def forward(p, k, chip, slot):
        sib_copy(p, k).wait_recv()
        part[c, p, k] = pair_sum(p, k).astype(BF)
        for h in range(2):
            z_copy(p, k, h, chip, slot).start()

    def merge(p, k, slot, chip):
        sib_copy(p, k).wait_recv()
        total = pair_sum(p, k)
        for h in range(2):
            z_arrival(p, slot, h)
            part[c, p, k, half(h)] = (total[half(h)] + zin[p, slot, half(h)].astype(F32)).astype(BF)
            z_copy(p, k, h, chip, 3).start()

    def kv_copy(m):
        return pltpu.make_async_remote_copy(
            src_ref=kv.at[s], dst_ref=kv.at[s],
            send_sem=kv_send.at[m], recv_sem=kv_recv.at[m],
            device_id=(peers[m], f), device_id_type=MESH,
        )

    def kv_arrival(m):
        pltpu.make_async_remote_copy(
            src_ref=kv.at[peers[m]], dst_ref=kv.at[peers[m]],
            send_sem=kv_send.at[m], recv_sem=kv_recv.at[m],
            device_id=(peers[m], f), device_id_type=MESH,
        ).wait_recv()

    def share_kv():
        sib_copy(0, 3).wait_recv()
        for slot in (2, 3):
            for h in range(2):
                z_arrival(0, slot, h)
        total = pair_sum(0, 3) + zin[0, 2].astype(F32) + zin[0, 3].astype(F32)
        kv[s] = total.astype(BF)

        @pl.when(is_end)
        def _():
            for h in range(2):
                z_arrival(0, 1, h)
            kv[s] = (total + zin[0, 1].astype(F32)).astype(BF)

        for m in range(3):
            kv_copy(m).start()

    def attend(p, h):
        for slot in (3, 2):
            z_arrival(p, slot, h)
        queries = (
            part[c, p, 3, half(h)].astype(F32) + sib[p, 3, half(h)].astype(F32)
            + zin[p, 3, half(h)].astype(F32) + zin[p, 2, half(h)].astype(F32)
        ).astype(BF)
        heads = jnp.concatenate([queries[:, :HD], queries[:, HD:]], axis=0)
        keys = kv[:, :, :HD].reshape(STRIPES * ROWS, HD)
        values = kv[:, :, HD:].reshape(STRIPES * ROWS, HD)
        scores = lax.dot_general(
            heads, keys, (((1,), (1,)), ((), ())), preferred_element_type=F32
        ) * HD ** (-0.5)
        masked = (
            scores.reshape(2, HALF, STRIPES * ROWS) + bias[half(h)][None]
        ).reshape(2 * HALF, STRIPES * ROWS)
        weights = jnp.exp(masked - jnp.max(masked, axis=1, keepdims=True))
        totals = jnp.sum(weights, axis=1, keepdims=True)
        result = (dot(weights.astype(BF), values) / totals).astype(BF)
        at = (p - 1) * WIDE
        o_ref[half(h), at : at + HD] = result[:HALF]
        o_ref[half(h), at + HD : at + WIDE] = result[HALF:]

    def project_queries(k):
        weight_copy(0, k).wait()
        for p in (1, 2):
            project(p, k)
            sib_copy(p, k).start()

    x_copy.wait()
    project(0, 0)
    pl.semaphore_wait(barrier, 7)
    sib_copy(0, 0).start()
    for k in (1, 2, 3):
        project(0, k)
        sib_copy(0, k).start()

    forward(0, 0, far_end + ends * (near - far_end), 3 - 3 * ends)
    project_queries(0)

    @pl.when(is_end)
    def _():
        forward(0, 1, far_end, 1)

    forward(0, 2, near, 2)
    project_queries(1)

    @pl.when(is_end)
    def _():
        forward(1, 0, near, 0)
        forward(2, 0, near, 0)

    project_queries(2)

    @pl.when(is_mid)
    def _():
        merge(0, 1, 0, far_mid)

    project_queries(3)

    @pl.when(is_end)
    def _():
        forward(1, 1, near, 1)
        forward(2, 1, near, 1)

    forward(1, 2, near, 2)
    forward(2, 2, near, 2)

    doc_copy.wait()
    tokens = STRIPES * ROWS
    by_pos = jnp.broadcast_to(doc[...], (8, tokens)).astype(BF)
    stored = lax.broadcasted_iota(jnp.int32, (tokens, tokens), 0)
    placed = lax.broadcasted_iota(jnp.int32, (tokens, tokens), 1)
    pick_keys = (placed == (stored & (ROWS - 1)) * STRIPES + (stored >> 7)).astype(F32).astype(BF)
    key_doc = lax.dot_general(
        by_pos, pick_keys, (((1,), (1,)), ((), ())), preferred_element_type=F32
    )[:1]
    mine = lax.broadcasted_iota(jnp.int32, (ROWS, tokens), 0) * STRIPES + s
    column = lax.broadcasted_iota(jnp.int32, (ROWS, tokens), 1)
    pick_rows = (column == mine).astype(F32).astype(BF)
    query_doc = lax.dot_general(
        pick_rows, by_pos, (((1,), (1,)), ((), ())), preferred_element_type=F32
    )[:, :1]
    key_pos = (column & (ROWS - 1)) * STRIPES + (column >> 7)
    allowed = (key_pos <= mine) & (key_doc == query_doc)
    bias[...] = jnp.where(allowed, 0.0, -1e30)

    share_kv()

    @pl.when(is_mid)
    def _():
        for k in range(2):
            for p in (1, 2):
                merge(p, k, k, q_order[k])

    for p in (1, 2):
        sib_copy(p, 3).wait_recv()
    for m in range(3):
        kv_arrival(m)
    for p in (1, 2):
        for h in range(2):
            attend(p, h)

    for p in range(PIECES):
        for k in range(CHIPS):
            sib_copy(p, k).wait_send()
    for p in range(PIECES):
        for k in range(3):
            for h in range(2):
                z_copy(p, k, h, near, 0).wait_send()
    for m in range(3):
        kv_copy(m).wait_send()


def fused(activations, query_weight, key_weight, value_weight, document_ids):
    depth = activations.shape[1]
    return pl.pallas_call(
        fused_kernel,
        out_shape=jax.ShapeDtypeStruct((ROWS, 4 * HD), BF),
        in_specs=[pl.BlockSpec(memory_space=pltpu.HBM)] * 5,
        out_specs=pl.BlockSpec(memory_space=pltpu.VMEM),
        scratch_shapes=[
            pltpu.VMEM((ROWS, depth), BF),
            pltpu.VMEM((1, STRIPES * ROWS), jnp.int32),
            pltpu.VMEM((CHIPS, depth, 1024), BF),
            pltpu.VMEM((CHIPS, depth, 256), BF),
            pltpu.VMEM((CHIPS, depth, 256), BF),
            pltpu.VMEM((2, PIECES, CHIPS, ROWS, WIDE), BF),
            pltpu.VMEM((PIECES, CHIPS, ROWS, WIDE), BF),
            pltpu.VMEM((PIECES, CHIPS, ROWS, WIDE), BF),
            pltpu.VMEM((STRIPES, ROWS, WIDE), BF),
            pltpu.VMEM((ROWS, STRIPES * ROWS), F32),
            pltpu.SemaphoreType.DMA((2,)),
            pltpu.SemaphoreType.DMA((3, CHIPS)),
            pltpu.SemaphoreType.DMA((PIECES, CHIPS)),
            pltpu.SemaphoreType.DMA((PIECES, CHIPS)),
            pltpu.SemaphoreType.DMA((PIECES, CHIPS, 2)),
            pltpu.SemaphoreType.DMA((PIECES, CHIPS, 2)),
            pltpu.SemaphoreType.DMA((3,)),
            pltpu.SemaphoreType.DMA((3,)),
        ],
        compiler_params=pltpu.CompilerParams(
            collective_id=0, has_side_effects=True, vmem_limit_bytes=60 * 1024 * 1024
        ),
    )(activations, document_ids.reshape(1, -1), query_weight, key_weight, value_weight)


def solution(mesh):
    small = mesh.shape["seq"] == STRIPES and mesh.shape["feat"] == 2 * CHIPS
    return jax.shard_map(
        fused if small else local,
        mesh=mesh,
        in_specs=(P("seq", "feat"), P("feat", None), P("feat", None), P("feat", None), P()),
        out_specs=P("seq", "feat"),
        check_vma=False,
    )
```

```python
import jax
import jax.numpy as jnp
from jax import lax
from jax.experimental import pallas as pl
from jax.experimental.pallas import tpu as pltpu
from jax.sharding import PartitionSpec as P

H = 32
KVH = 8
HD = 128


def passed_along(value, axis, steps):
    count = lax.axis_size(axis)
    pairs = [(source, (source + steps) % count) for source in range(count)]
    return lax.ppermute(value, axis, pairs)


def attend_block(
    softmax_state, kv_block, source, query_heads, query_pos, query_doc, doc_table, stripes
):
    maxima, totals, accumulated = softmax_state
    row_count = kv_block.shape[0]
    head_size = kv_block.shape[1] // 2
    key_rows = kv_block[:, :head_size]
    value_rows = kv_block[:, head_size:]
    key_pos = jnp.arange(row_count, dtype=jnp.int32) * stripes + source
    key_doc = lax.dynamic_slice_in_dim(doc_table, source, 1, 1)[:, 0]
    allowed = (key_pos[None, :] <= query_pos[:, None]) & (key_doc[None, :] == query_doc[:, None])
    scores = jnp.einsum(
        "qhd,kd->hqk", query_heads, key_rows, preferred_element_type=jnp.float32
    ) * head_size ** (-0.5)
    masked = jnp.where(allowed[None], scores, -1e30)
    newmax = jnp.maximum(maxima, jnp.max(masked, axis=2))
    weights = jnp.where(allowed[None], jnp.exp(scores - newmax[..., None]), 0.0)
    factor = jnp.exp(maxima - newmax)
    totals = totals * factor + jnp.sum(weights, axis=2)
    accumulated = accumulated * factor[..., None] + jnp.einsum(
        "hqk,kd->hqd", weights.astype(jnp.bfloat16), value_rows, preferred_element_type=jnp.float32
    )
    return (newmax, totals, accumulated)


def local(activations, query_weight, key_weight, value_weight, document_ids):
    row_count = activations.shape[0]
    features = lax.axis_size("feat")
    stripes = lax.axis_size("seq")
    seq_rank = lax.axis_index("seq")
    per_device = H // features
    group_size = H // KVH
    query_part = jnp.dot(activations, query_weight, preferred_element_type=jnp.float32).astype(
        jnp.bfloat16
    )
    key_part = jnp.dot(activations, key_weight, preferred_element_type=jnp.float32).astype(
        jnp.bfloat16
    )
    value_part = jnp.dot(activations, value_weight, preferred_element_type=jnp.float32).astype(
        jnp.bfloat16
    )
    owners = [rank * per_device // group_size for rank in range(features)]

    def by_owner(part):
        return jnp.stack([part[:, owner * HD : (owner + 1) * HD] for owner in owners], axis=1)

    stacked = jnp.concatenate(
        [
            query_part.reshape(row_count, features, per_device * HD),
            by_owner(key_part),
            by_owner(value_part),
        ],
        axis=2,
    ).reshape(row_count, features * (per_device + 2) * HD)
    summed = (
        lax.psum_scatter(stacked, "feat", scatter_dimension=1, tiled=True)
        .astype(jnp.float32)
        .astype(jnp.bfloat16)
    )
    queries = summed[:, : per_device * HD]
    kv_block = summed[:, per_device * HD :]
    query_heads = queries.reshape(row_count, per_device, HD)
    query_pos = jnp.arange(row_count, dtype=jnp.int32) * stripes + seq_rank
    doc_table = document_ids.reshape(row_count, stripes)
    query_doc = lax.dynamic_slice_in_dim(doc_table, seq_rank, 1, 1)[:, 0]

    def visit_block(running, current, source):
        return attend_block(
            running, current, source, query_heads, query_pos, query_doc, doc_table, stripes
        )

    softmax_state = (
        jnp.full((per_device, row_count), -1e30, jnp.float32),
        jnp.zeros((per_device, row_count), jnp.float32),
        jnp.zeros((per_device, row_count, HD), jnp.float32),
    )
    softmax_state = visit_block(softmax_state, kv_block, seq_rank)

    def advance(cycle_step, loop_carry):
        current, running = loop_carry
        current = passed_along(current, "seq", 1)
        return (current, visit_block(running, current, (seq_rank - cycle_step) % stripes))

    loop_carry = lax.fori_loop(1, stripes, advance, (kv_block, softmax_state))
    softmax_state = loop_carry[1]
    maxima, totals, accumulated = softmax_state
    output = (accumulated / totals[..., None]).astype(jnp.bfloat16)
    return output.transpose(1, 0, 2).reshape(row_count, per_device * HD)


MESH = pl.DeviceIdType.MESH
ROWS = 128
HALF = 64
WIDE = 256
PIECES = 3
CHIPS = 4
STRIPES = 4
BF = jnp.bfloat16
F32 = jnp.float32


def fused_kernel(
    x_hbm, doc_hbm, wq_hbm, wk_hbm, wv_hbm, o_ref,
    x, doc, wq, wk, wv, part, sib, zin, kv, bias,
    in_sem, w_sem, sib_send, sib_recv, z_send, z_recv, kv_send, kv_recv,
    line_sem, plane_sem, all_sem,
):
    s = lax.axis_index("seq")
    f = lax.axis_index("feat")
    z = f // 2
    c = f % 2
    other = 1 - c
    sibling = (s, f + 1 - 2 * c)
    right = z // 2
    end = 3 * right
    is_end = z == end
    is_mid = z != end
    ends = is_end.astype(jnp.int32)
    near = z + 1 - 2 * (z % 2)
    far_end = 3 - end
    far_mid = 2 - right
    q_order = (far_end, far_mid, near, z)
    kv_order = (
        far_end + ends * (far_mid - far_end), far_mid + ends * (far_end - far_mid), near, z,
    )
    peers = (s + 1 - 2 * (s % 2), s + 2 - 4 * (s // 2), 3 - s)

    is_hub = z == 1
    outward = (s, 2 * near + c)

    def signal(sem, device):
        pl.semaphore_signal(sem, inc=1, device_id=device, device_id_type=MESH)

    barrier = pltpu.get_barrier_semaphore()
    signal(barrier, sibling)
    signal(barrier, outward)

    @pl.when(is_mid)
    def _():
        signal(barrier, (s, 2 * (3 - z) + c))

    @pl.when(is_hub)
    def _():
        for peer in peers:
            signal(barrier, (peer, f))

    hub = is_hub.astype(jnp.int32)
    expected = 3 - ends + 3 * hub

    def weight_copy(kind, k):
        source, held, width = ((wq_hbm, wq, 1024), (wk_hbm, wk, 256), (wv_hbm, wv, 256))[kind]
        order = kv_order if kind else q_order
        at = pl.multiple_of(order[k] * width, 128)
        return pltpu.make_async_copy(source.at[:, pl.ds(at, width)], held.at[k], w_sem.at[kind, k])

    x_copy = pltpu.make_async_copy(x_hbm, x, in_sem.at[0])
    doc_copy = pltpu.make_async_copy(doc_hbm, doc, in_sem.at[1])
    x_copy.start()
    for k in range(CHIPS):
        weight_copy(1, k).start()
        weight_copy(2, k).start()

    def dot(a, b):
        return jnp.dot(a, b, preferred_element_type=F32)

    def sib_copy(p, k):
        return pltpu.make_async_remote_copy(
            src_ref=part.at[other, p, k], dst_ref=sib.at[p, k],
            send_sem=sib_send.at[p, k], recv_sem=sib_recv.at[p, k],
            device_id=sibling, device_id_type=MESH,
        )

    def project(p, k):
        rows = x[...]
        if p == 0:
            weight_copy(1, k).wait()
            weight_copy(2, k).wait()
            keys = dot(rows, wk[k]).astype(BF)
            values = dot(rows, wv[k]).astype(BF)
            for lane in range(2):
                part[lane, 0, k, :, :HD] = keys[:, lane * HD : (lane + 1) * HD]
                part[lane, 0, k, :, HD:] = values[:, lane * HD : (lane + 1) * HD]
        else:
            for lane in range(2):
                at = lane * 512 + (p - 1) * WIDE
                part[lane, p, k] = dot(rows, wq[k, :, at : at + WIDE]).astype(BF)

    def half(h):
        return slice(h * HALF, (h + 1) * HALF)

    def z_copy(p, k, h, chip, slot):
        return pltpu.make_async_remote_copy(
            src_ref=part.at[c, p, k, half(h)], dst_ref=zin.at[p, slot, half(h)],
            send_sem=z_send.at[p, k, h], recv_sem=z_recv.at[p, slot, h],
            device_id=(s, 2 * chip + c), device_id_type=MESH,
        )

    def z_arrival(p, slot, h):
        z_copy(p, 0, h, near, slot).wait_recv()

    def pair_sum(p, k):
        return part[c, p, k].astype(F32) + sib[p, k].astype(F32)

    def forward(p, k, chip, slot):
        sib_copy(p, k).wait_recv()
        part[c, p, k] = pair_sum(p, k).astype(BF)
        for h in range(2):
            z_copy(p, k, h, chip, slot).start()

    def merge(p, k, slot, chip):
        sib_copy(p, k).wait_recv()
        total = pair_sum(p, k)
        for h in range(2):
            z_arrival(p, slot, h)
            part[c, p, k, half(h)] = (total[half(h)] + zin[p, slot, half(h)].astype(F32)).astype(BF)
            z_copy(p, k, h, chip, 3).start()

    def kv_copy(m):
        return pltpu.make_async_remote_copy(
            src_ref=kv.at[s], dst_ref=kv.at[s],
            send_sem=kv_send.at[m], recv_sem=kv_recv.at[m],
            device_id=(peers[m], f), device_id_type=MESH,
        )

    def kv_arrival(m):
        pltpu.make_async_remote_copy(
            src_ref=kv.at[peers[m]], dst_ref=kv.at[peers[m]],
            send_sem=kv_send.at[m], recv_sem=kv_recv.at[m],
            device_id=(peers[m], f), device_id_type=MESH,
        ).wait_recv()

    def share_kv():
        sib_copy(0, 3).wait_recv()
        for slot in (2, 3):
            for h in range(2):
                z_arrival(0, slot, h)
        total = pair_sum(0, 3) + zin[0, 2].astype(F32) + zin[0, 3].astype(F32)
        kv[s] = total.astype(BF)

        @pl.when(is_end)
        def _():
            for h in range(2):
                z_arrival(0, 1, h)
            kv[s] = (total + zin[0, 1].astype(F32)).astype(BF)

        for m in range(3):
            kv_copy(m).start()

    def attend(p, h):
        for slot in (3, 2):
            z_arrival(p, slot, h)
        queries = (
            part[c, p, 3, half(h)].astype(F32) + sib[p, 3, half(h)].astype(F32)
            + zin[p, 3, half(h)].astype(F32) + zin[p, 2, half(h)].astype(F32)
        ).astype(BF)
        heads = jnp.concatenate([queries[:, :HD], queries[:, HD:]], axis=0)
        keys = kv[:, :, :HD].reshape(STRIPES * ROWS, HD)
        values = kv[:, :, HD:].reshape(STRIPES * ROWS, HD)
        scores = lax.dot_general(
            heads, keys, (((1,), (1,)), ((), ())), preferred_element_type=F32
        ) * HD ** (-0.5)
        masked = (
            scores.reshape(2, HALF, STRIPES * ROWS) + bias[half(h)][None]
        ).reshape(2 * HALF, STRIPES * ROWS)
        weights = jnp.exp(masked - jnp.max(masked, axis=1, keepdims=True))
        totals = jnp.sum(weights, axis=1, keepdims=True)
        result = (dot(weights.astype(BF), values) / totals).astype(BF)
        at = (p - 1) * WIDE
        o_ref[half(h), at : at + HD] = result[:HALF]
        o_ref[half(h), at + HD : at + WIDE] = result[HALF:]

    def project_queries(k):
        weight_copy(0, k).wait()
        for p in (1, 2):
            project(p, k)
            sib_copy(p, k).start()

    x_copy.wait()
    project(0, 0)
    weight_copy(0, 0).start()
    pl.semaphore_wait(barrier, expected)

    @pl.when(is_mid)
    def _():
        signal(line_sem, (s, 2 * (3 - z) + c))

    sib_copy(0, 0).start()
    for k in (1, 2, 3):
        project(0, k)
        sib_copy(0, k).start()
        weight_copy(0, k).start()
    doc_copy.start()

    @pl.when(is_end)
    def _():
        forward(0, 0, near, 0)

    @pl.when(is_mid)
    def _():
        forward(0, 2, near, 2)

    project_queries(0)
    pl.semaphore_wait(line_sem, 1)

    @pl.when(is_mid)
    def _():
        signal(line_sem, outward)
        forward(0, 0, far_end, 3)

    @pl.when(is_end)
    def _():
        forward(0, 1, far_end, 1)
        forward(0, 2, near, 2)

    @pl.when(is_hub)
    def _():
        for peer in peers:
            signal(plane_sem, (peer, f))

    project_queries(1)

    @pl.when(is_end)
    def _():
        forward(1, 0, near, 0)
        forward(2, 0, near, 0)

    project_queries(2)

    @pl.when(is_mid)
    def _():
        merge(0, 1, 0, far_mid)

    project_queries(3)

    @pl.when(is_end)
    def _():
        forward(1, 1, near, 1)
        forward(2, 1, near, 1)

    forward(1, 2, near, 2)
    forward(2, 2, near, 2)

    doc_copy.wait()
    tokens = STRIPES * ROWS
    by_pos = jnp.broadcast_to(doc[...], (8, tokens)).astype(BF)
    stored = lax.broadcasted_iota(jnp.int32, (tokens, tokens), 0)
    placed = lax.broadcasted_iota(jnp.int32, (tokens, tokens), 1)
    pick_keys = (placed == (stored & (ROWS - 1)) * STRIPES + (stored >> 7)).astype(F32).astype(BF)
    key_doc = lax.dot_general(
        by_pos, pick_keys, (((1,), (1,)), ((), ())), preferred_element_type=F32
    )[:1]
    mine = lax.broadcasted_iota(jnp.int32, (ROWS, tokens), 0) * STRIPES + s
    column = lax.broadcasted_iota(jnp.int32, (ROWS, tokens), 1)
    pick_rows = (column == mine).astype(F32).astype(BF)
    query_doc = lax.dot_general(
        pick_rows, by_pos, (((1,), (1,)), ((), ())), preferred_element_type=F32
    )[:, :1]
    key_pos = (column & (ROWS - 1)) * STRIPES + (column >> 7)
    allowed = (key_pos <= mine) & (key_doc == query_doc)
    bias[...] = jnp.where(allowed, 0.0, -1e30)

    @pl.when(is_hub)
    def _():
        pl.semaphore_wait(plane_sem, 3)
        signal(all_sem, (s, 2 * (3 - z) + c))
        signal(all_sem, outward)

    @pl.when(z != 1)
    def _():
        pl.semaphore_wait(all_sem, 1)

    @pl.when(z == 2)
    def _():
        signal(all_sem, outward)

    share_kv()

    @pl.when(is_mid)
    def _():
        for k in range(2):
            for p in (1, 2):
                merge(p, k, k, q_order[k])

    for p in (1, 2):
        sib_copy(p, 3).wait_recv()
    for m in range(3):
        kv_arrival(m)
    for p in (1, 2):
        for h in range(2):
            attend(p, h)

    for p in range(PIECES):
        for k in range(CHIPS):
            sib_copy(p, k).wait_send()
    for p in range(PIECES):
        for k in range(3):
            for h in range(2):
                z_copy(p, k, h, near, 0).wait_send()
    for m in range(3):
        kv_copy(m).wait_send()


def fused(activations, query_weight, key_weight, value_weight, document_ids):
    depth = activations.shape[1]
    operands = (
        activations, document_ids.reshape(1, -1), query_weight, key_weight, value_weight,
    )
    return pl.pallas_call(
        fused_kernel,
        out_shape=jax.ShapeDtypeStruct((ROWS, 4 * HD), BF),
        in_specs=[pl.BlockSpec(memory_space=pltpu.HBM)] * 5,
        out_specs=pl.BlockSpec(memory_space=pltpu.VMEM),
        scratch_shapes=[
            pltpu.VMEM((ROWS, depth), BF),
            pltpu.VMEM((1, STRIPES * ROWS), jnp.int32),
            pltpu.VMEM((CHIPS, depth, 1024), BF),
            pltpu.VMEM((CHIPS, depth, 256), BF),
            pltpu.VMEM((CHIPS, depth, 256), BF),
            pltpu.VMEM((2, PIECES, CHIPS, ROWS, WIDE), BF),
            pltpu.VMEM((PIECES, CHIPS, ROWS, WIDE), BF),
            pltpu.VMEM((PIECES, CHIPS, ROWS, WIDE), BF),
            pltpu.VMEM((STRIPES, ROWS, WIDE), BF),
            pltpu.VMEM((ROWS, STRIPES * ROWS), F32),
            pltpu.SemaphoreType.DMA((2,)),
            pltpu.SemaphoreType.DMA((3, CHIPS)),
            pltpu.SemaphoreType.DMA((PIECES, CHIPS)),
            pltpu.SemaphoreType.DMA((PIECES, CHIPS)),
            pltpu.SemaphoreType.DMA((PIECES, CHIPS, 2)),
            pltpu.SemaphoreType.DMA((PIECES, CHIPS, 2)),
            pltpu.SemaphoreType.DMA((3,)),
            pltpu.SemaphoreType.DMA((3,)),
            pltpu.SemaphoreType.REGULAR,
            pltpu.SemaphoreType.REGULAR,
            pltpu.SemaphoreType.REGULAR,
        ],
        compiler_params=pltpu.CompilerParams(
            collective_id=0, has_side_effects=True, vmem_limit_bytes=53 * 1024 * 1024
        ),
    )(*[pltpu.with_memory_space_constraint(operand, pltpu.HBM) for operand in operands])


def solution(mesh):
    small = mesh.shape["seq"] == STRIPES and mesh.shape["feat"] == 2 * CHIPS
    return jax.shard_map(
        fused if small else local,
        mesh=mesh,
        in_specs=(P("seq", "feat"), P("feat", None), P("feat", None), P("feat", None), P()),
        out_specs=P("seq", "feat"),
        check_vma=False,
    )
```

```python
import jax
import jax.numpy as jnp
from jax import lax
from jax.experimental import pallas as pl
from jax.experimental.pallas import tpu as pltpu
from jax.sharding import PartitionSpec as P

H = 32
KVH = 8
HD = 128


def passed_along(value, axis, steps):
    count = lax.axis_size(axis)
    pairs = [(source, (source + steps) % count) for source in range(count)]
    return lax.ppermute(value, axis, pairs)


def attend_block(
    softmax_state, kv_block, source, query_heads, query_pos, query_doc, doc_table, stripes
):
    maxima, totals, accumulated = softmax_state
    row_count = kv_block.shape[0]
    head_size = kv_block.shape[1] // 2
    key_rows = kv_block[:, :head_size]
    value_rows = kv_block[:, head_size:]
    key_pos = jnp.arange(row_count, dtype=jnp.int32) * stripes + source
    key_doc = lax.dynamic_slice_in_dim(doc_table, source, 1, 1)[:, 0]
    allowed = (key_pos[None, :] <= query_pos[:, None]) & (key_doc[None, :] == query_doc[:, None])
    scores = jnp.einsum(
        "qhd,kd->hqk", query_heads, key_rows, preferred_element_type=jnp.float32
    ) * head_size ** (-0.5)
    masked = jnp.where(allowed[None], scores, -1e30)
    newmax = jnp.maximum(maxima, jnp.max(masked, axis=2))
    weights = jnp.where(allowed[None], jnp.exp(scores - newmax[..., None]), 0.0)
    factor = jnp.exp(maxima - newmax)
    totals = totals * factor + jnp.sum(weights, axis=2)
    accumulated = accumulated * factor[..., None] + jnp.einsum(
        "hqk,kd->hqd", weights.astype(jnp.bfloat16), value_rows, preferred_element_type=jnp.float32
    )
    return (newmax, totals, accumulated)


def local(activations, query_weight, key_weight, value_weight, document_ids):
    row_count = activations.shape[0]
    features = lax.axis_size("feat")
    stripes = lax.axis_size("seq")
    seq_rank = lax.axis_index("seq")
    per_device = H // features
    group_size = H // KVH
    query_part = jnp.dot(activations, query_weight, preferred_element_type=jnp.float32).astype(
        jnp.bfloat16
    )
    key_part = jnp.dot(activations, key_weight, preferred_element_type=jnp.float32).astype(
        jnp.bfloat16
    )
    value_part = jnp.dot(activations, value_weight, preferred_element_type=jnp.float32).astype(
        jnp.bfloat16
    )
    owners = [rank * per_device // group_size for rank in range(features)]

    def by_owner(part):
        return jnp.stack([part[:, owner * HD : (owner + 1) * HD] for owner in owners], axis=1)

    stacked = jnp.concatenate(
        [
            query_part.reshape(row_count, features, per_device * HD),
            by_owner(key_part),
            by_owner(value_part),
        ],
        axis=2,
    ).reshape(row_count, features * (per_device + 2) * HD)
    summed = (
        lax.psum_scatter(stacked, "feat", scatter_dimension=1, tiled=True)
        .astype(jnp.float32)
        .astype(jnp.bfloat16)
    )
    queries = summed[:, : per_device * HD]
    kv_block = summed[:, per_device * HD :]
    query_heads = queries.reshape(row_count, per_device, HD)
    query_pos = jnp.arange(row_count, dtype=jnp.int32) * stripes + seq_rank
    doc_table = document_ids.reshape(row_count, stripes)
    query_doc = lax.dynamic_slice_in_dim(doc_table, seq_rank, 1, 1)[:, 0]

    def visit_block(running, current, source):
        return attend_block(
            running, current, source, query_heads, query_pos, query_doc, doc_table, stripes
        )

    softmax_state = (
        jnp.full((per_device, row_count), -1e30, jnp.float32),
        jnp.zeros((per_device, row_count), jnp.float32),
        jnp.zeros((per_device, row_count, HD), jnp.float32),
    )
    softmax_state = visit_block(softmax_state, kv_block, seq_rank)

    def advance(cycle_step, loop_carry):
        current, running = loop_carry
        current = passed_along(current, "seq", 1)
        return (current, visit_block(running, current, (seq_rank - cycle_step) % stripes))

    loop_carry = lax.fori_loop(1, stripes, advance, (kv_block, softmax_state))
    softmax_state = loop_carry[1]
    maxima, totals, accumulated = softmax_state
    output = (accumulated / totals[..., None]).astype(jnp.bfloat16)
    return output.transpose(1, 0, 2).reshape(row_count, per_device * HD)


MESH = pl.DeviceIdType.MESH
ROWS = 128
HALF = 64
WIDE = 256
PIECES = 3
CHIPS = 4
STRIPES = 4
BF = jnp.bfloat16
F32 = jnp.float32


def fused_kernel(
    x_hbm, doc_hbm, wq_hbm, wk_hbm, wv_hbm, o_ref,
    x, doc, wq, wkv, part, sib, zin, kv, bias,
    in_sem, wkv_sem, wq_sem, send_sem, sib_recv, z_recv, kv_recv,
    line_sem, plane_sem, all_sem,
):
    s = lax.axis_index("seq")
    f = lax.axis_index("feat")
    z = f // 2
    c = f % 2
    other = 1 - c
    sibling = (s, f + 1 - 2 * c)
    right = z // 2
    end = 3 * right
    is_end = z == end
    is_mid = z != end
    ends = is_end.astype(jnp.int32)
    near = z + 1 - 2 * (z % 2)
    far_end = 3 - end
    far_mid = 2 - right
    q_order = (far_end, far_mid, near, z)
    kv_order = (
        far_end + ends * (far_mid - far_end), far_mid + ends * (far_end - far_mid), near, z,
    )
    peers = (s + 1 - 2 * (s % 2), s + 2 - 4 * (s // 2), 3 - s)

    def kv_weights(k):
        at = pl.ds(pl.multiple_of(kv_order[k] * 256, 128), 256)
        return [
            pltpu.make_async_copy(source.at[:, at], wkv.at[k, :, i * 256 : i * 256 + 256], wkv_sem.at[k])
            for i, source in enumerate((wk_hbm, wv_hbm))
        ]

    def kv_weights_wait(k):
        pltpu.make_async_copy(wkv.at[k], wkv.at[k], wkv_sem.at[k]).wait()

    def q_weights(k):
        at = pl.ds(pl.multiple_of(q_order[k] * 1024, 128), 1024)
        return pltpu.make_async_copy(wq_hbm.at[:, at], wq.at[k], wq_sem.at[k])

    x_copy = pltpu.make_async_copy(x_hbm, x, in_sem.at[0])
    doc_copy = pltpu.make_async_copy(doc_hbm, doc, in_sem.at[1])
    x_copy.start()
    for k in range(CHIPS):
        for copy in kv_weights(k):
            copy.start()

    is_hub = z == 1
    outward = (s, 2 * near + c)

    def signal(sem, device):
        pl.semaphore_signal(sem, inc=1, device_id=device, device_id_type=MESH)

    barrier = pltpu.get_barrier_semaphore()
    signal(barrier, sibling)
    signal(barrier, outward)

    @pl.when(is_mid)
    def _():
        signal(barrier, (s, 2 * (3 - z) + c))

    @pl.when(is_hub)
    def _():
        for peer in peers:
            signal(barrier, (peer, f))

    hub = is_hub.astype(jnp.int32)
    expected = 3 - ends + 3 * hub

    def dot(a, b):
        return jnp.dot(a, b, preferred_element_type=F32)

    def sib_copy(q, k):
        pieces = pl.ds(1, 2) if q else pl.ds(0, 1)
        return pltpu.make_async_remote_copy(
            src_ref=part.at[other, pieces, k], dst_ref=sib.at[pieces, k],
            send_sem=send_sem, recv_sem=sib_recv.at[q, k],
            device_id=sibling, device_id_type=MESH,
        )

    def project_kv(k):
        products = dot(x[...], wkv[k]).astype(BF)
        for lane in range(2):
            for i in range(2):
                at = i * WIDE + lane * HD
                part[lane, 0, k, :, i * HD : (i + 1) * HD] = products[:, at : at + HD]

    def project_queries(k):
        q_weights(k).wait()
        rows = x[...]
        for p in (1, 2):
            for lane in range(2):
                at = lane * 512 + (p - 1) * WIDE
                part[lane, p, k] = dot(rows, wq[k, :, at : at + WIDE]).astype(BF)
        sib_copy(1, k).start()

    def half(h):
        return slice(h * HALF, (h + 1) * HALF)

    def cuts(p):
        return [half(0), half(1)] if p else [slice(0, ROWS)]

    def arrived(p, slot, h):
        return z_recv.at[(max(slot - 1, 0), 3 + 2 * slot + h, 11 + 2 * slot + h)[p]]

    def z_copy(p, k, h, chip, slot):
        rows = cuts(p)[h]
        return pltpu.make_async_remote_copy(
            src_ref=part.at[c, p, k, rows], dst_ref=zin.at[p, slot, rows],
            send_sem=send_sem, recv_sem=arrived(p, slot, h),
            device_id=(s, 2 * chip + c), device_id_type=MESH,
        )

    def z_arrival(p, slot, h=0):
        z_copy(p, 0, h, near, slot).wait_recv()

    def pair_sum(p, k):
        return part[c, p, k].astype(F32) + sib[p, k].astype(F32)

    def forward(q, k, chip, slot):
        sib_copy(q, k).wait_recv()
        pieces = (1, 2) if q else (0,)
        for p in pieces:
            part[c, p, k] = pair_sum(p, k).astype(BF)
            for h in range(len(cuts(p))):
                z_copy(p, k, h, chip, slot).start()

    def merge(q, k, slot, chip):
        sib_copy(q, k).wait_recv()
        pieces = (1, 2) if q else (0,)
        for p in pieces:
            total = pair_sum(p, k)
            for h, rows in enumerate(cuts(p)):
                z_arrival(p, slot, h)
                part[c, p, k, rows] = (total[rows] + zin[p, slot, rows].astype(F32)).astype(BF)
                z_copy(p, k, h, chip, 3).start()

    def kv_copy(m):
        return pltpu.make_async_remote_copy(
            src_ref=kv.at[s], dst_ref=kv.at[s],
            send_sem=send_sem, recv_sem=kv_recv,
            device_id=(peers[m], f), device_id_type=MESH,
        )

    def share_kv():
        sib_copy(0, 3).wait_recv()
        for slot in (2, 3):
            z_arrival(0, slot)
        total = pair_sum(0, 3) + zin[0, 2].astype(F32) + zin[0, 3].astype(F32)
        kv[s] = total.astype(BF)

        @pl.when(is_end)
        def _():
            z_arrival(0, 1)
            kv[s] = (total + zin[0, 1].astype(F32)).astype(BF)

        for m in range(3):
            kv_copy(m).start()

    def attend(p, h):
        for slot in (3, 2):
            z_arrival(p, slot, h)
        queries = (
            part[c, p, 3, half(h)].astype(F32) + sib[p, 3, half(h)].astype(F32)
            + zin[p, 3, half(h)].astype(F32) + zin[p, 2, half(h)].astype(F32)
        ).astype(BF)
        heads = jnp.concatenate([queries[:, :HD], queries[:, HD:]], axis=0)
        keys = kv[:, :, :HD].reshape(STRIPES * ROWS, HD)
        values = kv[:, :, HD:].reshape(STRIPES * ROWS, HD)
        scores = lax.dot_general(
            heads, keys, (((1,), (1,)), ((), ())), preferred_element_type=F32
        ) * HD ** (-0.5)
        masked = (
            scores.reshape(2, HALF, STRIPES * ROWS) + bias[half(h)][None]
        ).reshape(2 * HALF, STRIPES * ROWS)
        weights = jnp.exp(masked - jnp.max(masked, axis=1, keepdims=True))
        totals = jnp.sum(weights, axis=1, keepdims=True)
        result = (dot(weights.astype(BF), values) / totals).astype(BF)
        at = (p - 1) * WIDE
        o_ref[half(h), at : at + HD] = result[:HALF]
        o_ref[half(h), at + HD : at + WIDE] = result[HALF:]

    x_copy.wait()
    kv_weights_wait(0)
    project_kv(0)
    pl.semaphore_wait(barrier, expected)
    sib_copy(0, 0).start()
    q_weights(0).start()

    @pl.when(is_mid)
    def _():
        signal(line_sem, (s, 2 * (3 - z) + c))

    for k in (1, 2, 3):
        kv_weights_wait(k)
    for k in (1, 2, 3):
        project_kv(k)
    for k in (1, 2, 3):
        sib_copy(0, k).start()
    for k in (1, 2, 3):
        q_weights(k).start()
    doc_copy.start()

    @pl.when(is_end)
    def _():
        forward(0, 0, near, 0)

    @pl.when(is_mid)
    def _():
        forward(0, 2, near, 2)

    project_queries(0)
    pl.semaphore_wait(line_sem, 1)

    @pl.when(is_mid)
    def _():
        signal(line_sem, outward)
        forward(0, 0, far_end, 3)

    @pl.when(is_end)
    def _():
        forward(0, 1, far_end, 1)
        forward(0, 2, near, 2)

    @pl.when(is_hub)
    def _():
        for peer in peers:
            signal(plane_sem, (peer, f))

    project_queries(1)

    @pl.when(is_end)
    def _():
        forward(1, 0, near, 0)

    project_queries(2)

    @pl.when(is_mid)
    def _():
        merge(0, 1, 0, far_mid)

    project_queries(3)

    @pl.when(is_end)
    def _():
        forward(1, 1, near, 1)

    forward(1, 2, near, 2)

    doc_copy.wait()
    tokens = STRIPES * ROWS
    by_pos = jnp.broadcast_to(doc[...], (8, tokens)).astype(BF)
    stored = lax.broadcasted_iota(jnp.int32, (tokens, tokens), 0)
    placed = lax.broadcasted_iota(jnp.int32, (tokens, tokens), 1)
    pick_keys = (placed == (stored & (ROWS - 1)) * STRIPES + (stored >> 7)).astype(F32).astype(BF)
    key_doc = lax.dot_general(
        by_pos, pick_keys, (((1,), (1,)), ((), ())), preferred_element_type=F32
    )[:1]
    mine = lax.broadcasted_iota(jnp.int32, (ROWS, tokens), 0) * STRIPES + s
    column = lax.broadcasted_iota(jnp.int32, (ROWS, tokens), 1)
    pick_rows = (column == mine).astype(F32).astype(BF)
    query_doc = lax.dot_general(
        pick_rows, by_pos, (((1,), (1,)), ((), ())), preferred_element_type=F32
    )[:, :1]
    key_pos = (column & (ROWS - 1)) * STRIPES + (column >> 7)
    allowed = (key_pos <= mine) & (key_doc == query_doc)
    bias[...] = jnp.where(allowed, 0.0, -1e30)

    @pl.when(is_hub)
    def _():
        pl.semaphore_wait(plane_sem, 3)
        signal(all_sem, (s, 2 * (3 - z) + c))
        signal(all_sem, outward)

    @pl.when(z != 1)
    def _():
        pl.semaphore_wait(all_sem, 1)

    @pl.when(z == 2)
    def _():
        signal(all_sem, outward)

    share_kv()

    @pl.when(is_mid)
    def _():
        for k in range(2):
            merge(1, k, k, q_order[k])

    sib_copy(1, 3).wait_recv()
    pltpu.make_async_copy(kv.at[pl.ds(0, 3)], kv.at[pl.ds(0, 3)], kv_recv).wait()
    for p in (1, 2):
        for h in range(2):
            attend(p, h)

    pltpu.make_async_copy(part, part, send_sem).wait()


def fused(activations, query_weight, key_weight, value_weight, document_ids):
    depth = activations.shape[1]
    operands = (
        activations, document_ids.reshape(1, -1), query_weight, key_weight, value_weight,
    )
    return pl.pallas_call(
        fused_kernel,
        out_shape=jax.ShapeDtypeStruct((ROWS, 4 * HD), BF),
        in_specs=[pl.BlockSpec(memory_space=pltpu.HBM)] * 5,
        out_specs=pl.BlockSpec(memory_space=pltpu.VMEM),
        scratch_shapes=[
            pltpu.VMEM((ROWS, depth), BF),
            pltpu.VMEM((1, STRIPES * ROWS), jnp.int32),
            pltpu.VMEM((CHIPS, depth, 1024), BF),
            pltpu.VMEM((CHIPS, depth, 512), BF),
            pltpu.VMEM((2, PIECES, CHIPS, ROWS, WIDE), BF),
            pltpu.VMEM((PIECES, CHIPS, ROWS, WIDE), BF),
            pltpu.VMEM((PIECES, CHIPS, ROWS, WIDE), BF),
            pltpu.VMEM((STRIPES, ROWS, WIDE), BF),
            pltpu.VMEM((ROWS, STRIPES * ROWS), F32),
            pltpu.SemaphoreType.DMA((2,)),
            pltpu.SemaphoreType.DMA((CHIPS,)),
            pltpu.SemaphoreType.DMA((CHIPS,)),
            pltpu.SemaphoreType.DMA,
            pltpu.SemaphoreType.DMA((2, CHIPS)),
            pltpu.SemaphoreType.DMA((19,)),
            pltpu.SemaphoreType.DMA,
            pltpu.SemaphoreType.REGULAR,
            pltpu.SemaphoreType.REGULAR,
            pltpu.SemaphoreType.REGULAR,
        ],
        compiler_params=pltpu.CompilerParams(
            collective_id=0, has_side_effects=True, vmem_limit_bytes=53 * 1024 * 1024
        ),
    )(*[pltpu.with_memory_space_constraint(operand, pltpu.HBM) for operand in operands])


def solution(mesh):
    small = mesh.shape["seq"] == STRIPES and mesh.shape["feat"] == 2 * CHIPS
    return jax.shard_map(
        fused if small else local,
        mesh=mesh,
        in_specs=(P("seq", "feat"), P("feat", None), P("feat", None), P("feat", None), P()),
        out_specs=P("seq", "feat"),
        check_vma=False,
    )
```

```python
import jax
import jax.numpy as jnp
from jax import lax
from jax.experimental import pallas as pl
from jax.experimental.pallas import tpu as pltpu
from jax.sharding import PartitionSpec as P

H = 32
KVH = 8
HD = 128


def passed_along(value, axis, steps):
    count = lax.axis_size(axis)
    pairs = [(source, (source + steps) % count) for source in range(count)]
    return lax.ppermute(value, axis, pairs)


def attend_block(
    softmax_state, kv_block, source, query_heads, query_pos, query_doc, doc_table, stripes
):
    maxima, totals, accumulated = softmax_state
    row_count = kv_block.shape[0]
    head_size = kv_block.shape[1] // 2
    key_rows = kv_block[:, :head_size]
    value_rows = kv_block[:, head_size:]
    key_pos = jnp.arange(row_count, dtype=jnp.int32) * stripes + source
    key_doc = lax.dynamic_slice_in_dim(doc_table, source, 1, 1)[:, 0]
    allowed = (key_pos[None, :] <= query_pos[:, None]) & (key_doc[None, :] == query_doc[:, None])
    scores = jnp.einsum(
        "qhd,kd->hqk", query_heads, key_rows, preferred_element_type=jnp.float32
    ) * head_size ** (-0.5)
    masked = jnp.where(allowed[None], scores, -1e30)
    newmax = jnp.maximum(maxima, jnp.max(masked, axis=2))
    weights = jnp.where(allowed[None], jnp.exp(scores - newmax[..., None]), 0.0)
    factor = jnp.exp(maxima - newmax)
    totals = totals * factor + jnp.sum(weights, axis=2)
    accumulated = accumulated * factor[..., None] + jnp.einsum(
        "hqk,kd->hqd", weights.astype(jnp.bfloat16), value_rows, preferred_element_type=jnp.float32
    )
    return (newmax, totals, accumulated)


def local(activations, query_weight, key_weight, value_weight, document_ids):
    row_count = activations.shape[0]
    features = lax.axis_size("feat")
    stripes = lax.axis_size("seq")
    seq_rank = lax.axis_index("seq")
    per_device = H // features
    group_size = H // KVH
    query_part = jnp.dot(activations, query_weight, preferred_element_type=jnp.float32).astype(
        jnp.bfloat16
    )
    key_part = jnp.dot(activations, key_weight, preferred_element_type=jnp.float32).astype(
        jnp.bfloat16
    )
    value_part = jnp.dot(activations, value_weight, preferred_element_type=jnp.float32).astype(
        jnp.bfloat16
    )
    owners = [rank * per_device // group_size for rank in range(features)]

    def by_owner(part):
        return jnp.stack([part[:, owner * HD : (owner + 1) * HD] for owner in owners], axis=1)

    stacked = jnp.concatenate(
        [
            query_part.reshape(row_count, features, per_device * HD),
            by_owner(key_part),
            by_owner(value_part),
        ],
        axis=2,
    ).reshape(row_count, features * (per_device + 2) * HD)
    summed = (
        lax.psum_scatter(stacked, "feat", scatter_dimension=1, tiled=True)
        .astype(jnp.float32)
        .astype(jnp.bfloat16)
    )
    queries = summed[:, : per_device * HD]
    kv_block = summed[:, per_device * HD :]
    query_heads = queries.reshape(row_count, per_device, HD)
    query_pos = jnp.arange(row_count, dtype=jnp.int32) * stripes + seq_rank
    doc_table = document_ids.reshape(row_count, stripes)
    query_doc = lax.dynamic_slice_in_dim(doc_table, seq_rank, 1, 1)[:, 0]

    def visit_block(running, current, source):
        return attend_block(
            running, current, source, query_heads, query_pos, query_doc, doc_table, stripes
        )

    softmax_state = (
        jnp.full((per_device, row_count), -1e30, jnp.float32),
        jnp.zeros((per_device, row_count), jnp.float32),
        jnp.zeros((per_device, row_count, HD), jnp.float32),
    )
    softmax_state = visit_block(softmax_state, kv_block, seq_rank)

    def advance(cycle_step, loop_carry):
        current, running = loop_carry
        current = passed_along(current, "seq", 1)
        return (current, visit_block(running, current, (seq_rank - cycle_step) % stripes))

    loop_carry = lax.fori_loop(1, stripes, advance, (kv_block, softmax_state))
    softmax_state = loop_carry[1]
    maxima, totals, accumulated = softmax_state
    output = (accumulated / totals[..., None]).astype(jnp.bfloat16)
    return output.transpose(1, 0, 2).reshape(row_count, per_device * HD)


MESH = pl.DeviceIdType.MESH
ROWS = 128
HALF = 64
WIDE = 256
PIECES = 3
CHIPS = 4
STRIPES = 4
BF = jnp.bfloat16
F32 = jnp.float32


def fused_kernel(
    x_hbm, doc_hbm, wq_hbm, wk_hbm, wv_hbm, o_ref,
    x, doc, wq, wkv, part, sib, zin, kv, bias,
    in_sem, wkv_sem, wq_sem, send_sem, sib_recv, raw_recv, z_recv, kv_recv,
    line_sem, plane_sem, all_sem,
):
    s = lax.axis_index("seq")
    f = lax.axis_index("feat")
    z = f // 2
    c = f % 2
    other = 1 - c
    sibling = (s, f + 1 - 2 * c)
    right = z // 2
    end = 3 * right
    is_end = z == end
    is_mid = z != end
    ends = is_end.astype(jnp.int32)
    near = z + 1 - 2 * (z % 2)
    far_end = 3 - end
    far_mid = 2 - right
    q_order = (far_end, far_mid, near, z)
    kv_order = (
        far_end + ends * (far_mid - far_end), far_mid + ends * (far_end - far_mid), near, z,
    )
    peers = (s + 1 - 2 * (s % 2), s + 2 - 4 * (s // 2), 3 - s)

    def kv_weights(k):
        at = pl.ds(pl.multiple_of(kv_order[k] * 256, 128), 256)
        return [
            pltpu.make_async_copy(source.at[:, at], wkv.at[k, :, i * 256 : i * 256 + 256], wkv_sem.at[k])
            for i, source in enumerate((wk_hbm, wv_hbm))
        ]

    def kv_weights_wait(k):
        pltpu.make_async_copy(wkv.at[k], wkv.at[k], wkv_sem.at[k]).wait()

    def q_weights(k):
        at = pl.ds(pl.multiple_of(q_order[k] * 1024, 128), 1024)
        return pltpu.make_async_copy(wq_hbm.at[:, at], wq.at[k], wq_sem.at[k])

    x_copy = pltpu.make_async_copy(x_hbm, x, in_sem.at[0])
    doc_copy = pltpu.make_async_copy(doc_hbm, doc, in_sem.at[1])
    x_copy.start()
    for k in range(CHIPS):
        for copy in kv_weights(k):
            copy.start()

    is_hub = z == 1
    outward = (s, 2 * near + c)

    def signal(sem, device):
        pl.semaphore_signal(sem, inc=1, device_id=device, device_id_type=MESH)

    barrier = pltpu.get_barrier_semaphore()
    signal(barrier, sibling)
    signal(barrier, outward)

    @pl.when(is_mid)
    def _():
        signal(barrier, (s, 2 * near + other))
        signal(barrier, (s, 2 * (3 - z) + c))

    @pl.when(is_hub)
    def _():
        for peer in peers:
            signal(barrier, (peer, f))

    hub = is_hub.astype(jnp.int32)
    expected = 3 + 3 * hub

    def dot(a, b):
        return jnp.dot(a, b, preferred_element_type=F32)

    def sib_copy(q, k):
        pieces = pl.ds(1, 2) if q else pl.ds(0, 1)
        return pltpu.make_async_remote_copy(
            src_ref=part.at[other, pieces, k], dst_ref=sib.at[pieces, k],
            send_sem=send_sem, recv_sem=sib_recv.at[q, k],
            device_id=sibling, device_id_type=MESH,
        )

    def raw_copy(i):
        lane = (c, other)[i]
        return pltpu.make_async_remote_copy(
            src_ref=part.at[lane, 0, 0, :, :HD], dst_ref=zin.at[0, i, :, :HD],
            send_sem=send_sem, recv_sem=raw_recv.at[i],
            device_id=(s, 2 * near + lane), device_id_type=MESH,
        )

    def first_sib_copy():
        return pltpu.make_async_remote_copy(
            src_ref=part.at[other, 0, 0, :, HD:], dst_ref=sib.at[0, 0, :, HD:],
            send_sem=send_sem, recv_sem=sib_recv.at[0, 0],
            device_id=sibling, device_id_type=MESH,
        )

    def first_z_copy():
        return pltpu.make_async_remote_copy(
            src_ref=part.at[c, 0, 0, :, HD:], dst_ref=zin.at[0, 0, :, HD:],
            send_sem=send_sem, recv_sem=arrived(0, 0, 0),
            device_id=outward, device_id_type=MESH,
        )

    def forward_first():
        first_sib_copy().wait_recv()
        part[c, 0, 0, :, HD:] = (
            part[c, 0, 0, :, HD:].astype(F32) + sib[0, 0, :, HD:].astype(F32)
        ).astype(BF)
        first_z_copy().start()

    def merge_first():
        sib_copy(0, 1).wait_recv()
        total = pair_sum(0, 1)
        for i in range(2):
            raw_copy(i).wait_recv()
        first_z_copy().wait_recv()
        part[c, 0, 1, :, :HD] = (
            total[:, :HD] + zin[0, 0, :, :HD].astype(F32) + zin[0, 1, :, :HD].astype(F32)
        ).astype(BF)
        part[c, 0, 1, :, HD:] = (total[:, HD:] + zin[0, 0, :, HD:].astype(F32)).astype(BF)
        z_copy(0, 1, 0, far_mid, 3).start()

    def project_kv(k):
        products = dot(x[...], wkv[k]).astype(BF)
        for lane in range(2):
            for i in range(2):
                at = i * WIDE + lane * HD
                part[lane, 0, k, :, i * HD : (i + 1) * HD] = products[:, at : at + HD]

    def project_queries(k):
        q_weights(k).wait()
        rows = x[...]
        for p in (1, 2):
            for lane in range(2):
                at = lane * 512 + (p - 1) * WIDE
                part[lane, p, k] = dot(rows, wq[k, :, at : at + WIDE]).astype(BF)
        sib_copy(1, k).start()

    def half(h):
        return slice(h * HALF, (h + 1) * HALF)

    def cuts(p):
        return [half(0), half(1)] if p else [slice(0, ROWS)]

    def arrived(p, slot, h):
        return z_recv.at[(max(slot - 1, 0), 3 + 2 * slot + h, 11 + 2 * slot + h)[p]]

    def z_copy(p, k, h, chip, slot):
        rows = cuts(p)[h]
        return pltpu.make_async_remote_copy(
            src_ref=part.at[c, p, k, rows], dst_ref=zin.at[p, slot, rows],
            send_sem=send_sem, recv_sem=arrived(p, slot, h),
            device_id=(s, 2 * chip + c), device_id_type=MESH,
        )

    def z_arrival(p, slot, h=0):
        z_copy(p, 0, h, near, slot).wait_recv()

    def pair_sum(p, k):
        return part[c, p, k].astype(F32) + sib[p, k].astype(F32)

    def forward(q, k, chip, slot):
        sib_copy(q, k).wait_recv()
        pieces = (1, 2) if q else (0,)
        for p in pieces:
            part[c, p, k] = pair_sum(p, k).astype(BF)
            for h in range(len(cuts(p))):
                z_copy(p, k, h, chip, slot).start()

    def merge(q, k, slot, chip):
        sib_copy(q, k).wait_recv()
        pieces = (1, 2) if q else (0,)
        for p in pieces:
            total = pair_sum(p, k)
            for h, rows in enumerate(cuts(p)):
                z_arrival(p, slot, h)
                part[c, p, k, rows] = (total[rows] + zin[p, slot, rows].astype(F32)).astype(BF)
                z_copy(p, k, h, chip, 3).start()

    def kv_copies(i):
        return [
            pltpu.make_async_remote_copy(
                src_ref=kv.at[i, s], dst_ref=kv.at[i, s],
                send_sem=send_sem, recv_sem=kv_recv.at[i],
                device_id=(peer, f), device_id_type=MESH,
            )
            for peer in peers[::-1]
        ]

    def kv_arrival(i):
        pltpu.make_async_copy(kv.at[i, pl.ds(0, 3)], kv.at[i, pl.ds(0, 3)], kv_recv.at[i]).wait()

    def share_kv():
        sib_copy(0, 3).wait_recv()
        for slot in (2, 3):
            z_arrival(0, slot)

        @pl.when(is_end)
        def _():
            z_arrival(0, 1)

        for i in range(2):
            at = slice(i * HD, (i + 1) * HD)
            total = (
                part[c, 0, 3, :, at].astype(F32) + sib[0, 3, :, at].astype(F32)
                + zin[0, 2, :, at].astype(F32) + zin[0, 3, :, at].astype(F32)
            )
            further = jnp.where(is_end, zin[0, 1, :, at].astype(F32), 0.0)
            kv[i, s] = (total + further).astype(BF)
            for copy in kv_copies(i):
                copy.start()

    def weigh(p, h):
        for slot in (3, 2):
            z_arrival(p, slot, h)
        queries = (
            part[c, p, 3, half(h)].astype(F32) + sib[p, 3, half(h)].astype(F32)
            + zin[p, 3, half(h)].astype(F32) + zin[p, 2, half(h)].astype(F32)
        ).astype(BF)
        heads = jnp.concatenate([queries[:, :HD], queries[:, HD:]], axis=0)
        keys = kv[0].reshape(STRIPES * ROWS, HD)
        scores = lax.dot_general(
            heads, keys, (((1,), (1,)), ((), ())), preferred_element_type=F32
        ) * HD ** (-0.5)
        masked = (
            scores.reshape(2, HALF, STRIPES * ROWS) + bias[half(h)][None]
        ).reshape(2 * HALF, STRIPES * ROWS)
        weights = jnp.exp(masked - jnp.max(masked, axis=1, keepdims=True))
        return weights.astype(BF), jnp.sum(weights, axis=1, keepdims=True)

    def attend(p, h, weighed):
        rounded, totals = weighed
        values = kv[1].reshape(STRIPES * ROWS, HD)
        result = (dot(rounded, values) / totals).astype(BF)
        at = (p - 1) * WIDE
        o_ref[half(h), at : at + HD] = result[:HALF]
        o_ref[half(h), at + HD : at + WIDE] = result[HALF:]

    x_copy.wait()
    kv_weights_wait(0)
    project_kv(0)
    pl.semaphore_wait(barrier, expected)

    @pl.when(is_end)
    def _():
        for i in range(2):
            raw_copy(i).start()
        first_sib_copy().start()

    @pl.when(is_mid)
    def _():
        sib_copy(0, 0).start()

    q_weights(0).start()

    @pl.when(is_mid)
    def _():
        signal(line_sem, (s, 2 * (3 - z) + c))

    for k in (1, 2, 3):
        kv_weights_wait(k)
    for k in (1, 2, 3):
        project_kv(k)
    for k in (1, 2, 3):
        sib_copy(0, k).start()
    for k in (1, 2, 3):
        q_weights(k).start()
    doc_copy.start()

    @pl.when(is_mid)
    def _():
        pl.semaphore_wait(line_sem, 1)
        signal(line_sem, outward)
        forward(0, 2, near, 2)

    @pl.when(is_end)
    def _():
        forward_first()

    @pl.when(z == 0)
    def _():
        forward(0, 2, near, 2)

    project_queries(0)

    @pl.when(z == 3)
    def _():
        pl.semaphore_wait(line_sem, 1)
        forward(0, 1, far_end, 1)
        forward(0, 2, near, 2)

    @pl.when(is_mid)
    def _():
        forward(0, 0, far_end, 3)

    @pl.when(is_hub)
    def _():
        for peer in peers:
            signal(plane_sem, (peer, f))

    project_queries(1)

    @pl.when(is_end)
    def _():
        forward(1, 0, near, 0)

    @pl.when(z == 0)
    def _():
        pl.semaphore_wait(line_sem, 1)
        forward(0, 1, far_end, 1)

    project_queries(2)
    project_queries(3)

    @pl.when(is_end)
    def _():
        forward(1, 1, near, 1)

    forward(1, 2, near, 2)

    doc_copy.wait()
    tokens = STRIPES * ROWS
    by_pos = jnp.broadcast_to(doc[...], (8, tokens)).astype(BF)
    stored = lax.broadcasted_iota(jnp.int32, (tokens, tokens), 0)
    placed = lax.broadcasted_iota(jnp.int32, (tokens, tokens), 1)
    pick_keys = (placed == (stored & (ROWS - 1)) * STRIPES + (stored >> 7)).astype(F32).astype(BF)
    key_doc = lax.dot_general(
        by_pos, pick_keys, (((1,), (1,)), ((), ())), preferred_element_type=F32
    )[:1]
    mine = lax.broadcasted_iota(jnp.int32, (ROWS, tokens), 0) * STRIPES + s
    column = lax.broadcasted_iota(jnp.int32, (ROWS, tokens), 1)
    pick_rows = (column == mine).astype(F32).astype(BF)
    query_doc = lax.dot_general(
        pick_rows, by_pos, (((1,), (1,)), ((), ())), preferred_element_type=F32
    )[:, :1]
    key_pos = (column & (ROWS - 1)) * STRIPES + (column >> 7)
    allowed = (key_pos <= mine) & (key_doc == query_doc)
    bias[...] = jnp.where(allowed, 0.0, -1e30)

    @pl.when(is_mid)
    def _():
        merge_first()

    @pl.when(is_hub)
    def _():
        pl.semaphore_wait(plane_sem, 3)
        signal(all_sem, (s, 2 * (3 - z) + c))
        signal(all_sem, outward)

    @pl.when(z != 1)
    def _():
        pl.semaphore_wait(all_sem, 1)

    @pl.when(z == 2)
    def _():
        signal(all_sem, outward)

    share_kv()

    @pl.when(is_mid)
    def _():
        for k in range(2):
            merge(1, k, k, q_order[k])

    sib_copy(1, 3).wait_recv()
    kv_arrival(0)
    early = [weigh(1, h) for h in range(2)]
    kv_arrival(1)
    for h in range(2):
        attend(1, h, early[h])
    for h in range(2):
        attend(2, h, weigh(2, h))

    pltpu.make_async_copy(part, part, send_sem).wait()


def fused(activations, query_weight, key_weight, value_weight, document_ids):
    depth = activations.shape[1]
    operands = (
        activations, document_ids.reshape(1, -1), query_weight, key_weight, value_weight,
    )
    return pl.pallas_call(
        fused_kernel,
        out_shape=jax.ShapeDtypeStruct((ROWS, 4 * HD), BF),
        in_specs=[pl.BlockSpec(memory_space=pltpu.HBM)] * 5,
        out_specs=pl.BlockSpec(memory_space=pltpu.VMEM),
        scratch_shapes=[
            pltpu.VMEM((ROWS, depth), BF),
            pltpu.VMEM((1, STRIPES * ROWS), jnp.int32),
            pltpu.VMEM((CHIPS, depth, 1024), BF),
            pltpu.VMEM((CHIPS, depth, 512), BF),
            pltpu.VMEM((2, PIECES, CHIPS, ROWS, WIDE), BF),
            pltpu.VMEM((PIECES, CHIPS, ROWS, WIDE), BF),
            pltpu.VMEM((PIECES, CHIPS, ROWS, WIDE), BF),
            pltpu.VMEM((2, STRIPES, ROWS, HD), BF),
            pltpu.VMEM((ROWS, STRIPES * ROWS), F32),
            pltpu.SemaphoreType.DMA((2,)),
            pltpu.SemaphoreType.DMA((CHIPS,)),
            pltpu.SemaphoreType.DMA((CHIPS,)),
            pltpu.SemaphoreType.DMA,
            pltpu.SemaphoreType.DMA((2, CHIPS)),
            pltpu.SemaphoreType.DMA((2,)),
            pltpu.SemaphoreType.DMA((19,)),
            pltpu.SemaphoreType.DMA((2,)),
            pltpu.SemaphoreType.REGULAR,
            pltpu.SemaphoreType.REGULAR,
            pltpu.SemaphoreType.REGULAR,
        ],
        compiler_params=pltpu.CompilerParams(
            collective_id=0, has_side_effects=True, vmem_limit_bytes=53 * 1024 * 1024
        ),
    )(*[pltpu.with_memory_space_constraint(operand, pltpu.HBM) for operand in operands])


def solution(mesh):
    small = mesh.shape["seq"] == STRIPES and mesh.shape["feat"] == 2 * CHIPS
    return jax.shard_map(
        fused if small else local,
        mesh=mesh,
        in_specs=(P("seq", "feat"), P("feat", None), P("feat", None), P("feat", None), P()),
        out_specs=P("seq", "feat"),
        check_vma=False,
    )
```

```python
import jax
import jax.numpy as jnp
from jax import lax
from jax.experimental import pallas as pl
from jax.experimental.pallas import tpu as pltpu
from jax.sharding import PartitionSpec as P

H = 32
KVH = 8
HD = 128


def passed_along(value, axis, steps):
    count = lax.axis_size(axis)
    pairs = [(source, (source + steps) % count) for source in range(count)]
    return lax.ppermute(value, axis, pairs)


def attend_block(
    softmax_state, kv_block, source, query_heads, query_pos, query_doc, doc_table, stripes
):
    maxima, totals, accumulated = softmax_state
    row_count = kv_block.shape[0]
    head_size = kv_block.shape[1] // 2
    key_rows = kv_block[:, :head_size]
    value_rows = kv_block[:, head_size:]
    key_pos = jnp.arange(row_count, dtype=jnp.int32) * stripes + source
    key_doc = lax.dynamic_slice_in_dim(doc_table, source, 1, 1)[:, 0]
    allowed = (key_pos[None, :] <= query_pos[:, None]) & (key_doc[None, :] == query_doc[:, None])
    scores = jnp.einsum(
        "qhd,kd->hqk", query_heads, key_rows, preferred_element_type=jnp.float32
    ) * head_size ** (-0.5)
    masked = jnp.where(allowed[None], scores, -1e30)
    newmax = jnp.maximum(maxima, jnp.max(masked, axis=2))
    weights = jnp.where(allowed[None], jnp.exp(scores - newmax[..., None]), 0.0)
    factor = jnp.exp(maxima - newmax)
    totals = totals * factor + jnp.sum(weights, axis=2)
    accumulated = accumulated * factor[..., None] + jnp.einsum(
        "hqk,kd->hqd", weights.astype(jnp.bfloat16), value_rows, preferred_element_type=jnp.float32
    )
    return (newmax, totals, accumulated)


def local(activations, query_weight, key_weight, value_weight, document_ids):
    row_count = activations.shape[0]
    features = lax.axis_size("feat")
    stripes = lax.axis_size("seq")
    seq_rank = lax.axis_index("seq")
    per_device = H // features
    group_size = H // KVH
    query_part = jnp.dot(activations, query_weight, preferred_element_type=jnp.float32).astype(
        jnp.bfloat16
    )
    key_part = jnp.dot(activations, key_weight, preferred_element_type=jnp.float32).astype(
        jnp.bfloat16
    )
    value_part = jnp.dot(activations, value_weight, preferred_element_type=jnp.float32).astype(
        jnp.bfloat16
    )
    owners = [rank * per_device // group_size for rank in range(features)]

    def by_owner(part):
        return jnp.stack([part[:, owner * HD : (owner + 1) * HD] for owner in owners], axis=1)

    stacked = jnp.concatenate(
        [
            query_part.reshape(row_count, features, per_device * HD),
            by_owner(key_part),
            by_owner(value_part),
        ],
        axis=2,
    ).reshape(row_count, features * (per_device + 2) * HD)
    summed = (
        lax.psum_scatter(stacked, "feat", scatter_dimension=1, tiled=True)
        .astype(jnp.float32)
        .astype(jnp.bfloat16)
    )
    queries = summed[:, : per_device * HD]
    kv_block = summed[:, per_device * HD :]
    query_heads = queries.reshape(row_count, per_device, HD)
    query_pos = jnp.arange(row_count, dtype=jnp.int32) * stripes + seq_rank
    doc_table = document_ids.reshape(row_count, stripes)
    query_doc = lax.dynamic_slice_in_dim(doc_table, seq_rank, 1, 1)[:, 0]

    def visit_block(running, current, source):
        return attend_block(
            running, current, source, query_heads, query_pos, query_doc, doc_table, stripes
        )

    softmax_state = (
        jnp.full((per_device, row_count), -1e30, jnp.float32),
        jnp.zeros((per_device, row_count), jnp.float32),
        jnp.zeros((per_device, row_count, HD), jnp.float32),
    )
    softmax_state = visit_block(softmax_state, kv_block, seq_rank)

    def advance(cycle_step, loop_carry):
        current, running = loop_carry
        current = passed_along(current, "seq", 1)
        return (current, visit_block(running, current, (seq_rank - cycle_step) % stripes))

    loop_carry = lax.fori_loop(1, stripes, advance, (kv_block, softmax_state))
    softmax_state = loop_carry[1]
    maxima, totals, accumulated = softmax_state
    output = (accumulated / totals[..., None]).astype(jnp.bfloat16)
    return output.transpose(1, 0, 2).reshape(row_count, per_device * HD)


MESH = pl.DeviceIdType.MESH
ROWS = 128
HALF = 64
WIDE = 256
PIECES = 3
CHIPS = 4
STRIPES = 4
BF = jnp.bfloat16
F32 = jnp.float32


def fused_kernel(
    x_hbm, doc_hbm, wq_hbm, wk_hbm, wv_hbm, o_ref,
    x, doc, wq, wkv, part, sib, zin, kv, bias,
    in_sem, wkv_sem, wq_sem, send_sem, sib_recv, raw_recv, z_recv, kv_recv,
    line_sem, plane_sem, all_sem,
):
    s = lax.axis_index("seq")
    f = lax.axis_index("feat")
    z = f // 2
    c = f % 2
    other = 1 - c
    sibling = (s, f + 1 - 2 * c)
    right = z // 2
    end = 3 * right
    is_end = z == end
    is_mid = z != end
    ends = is_end.astype(jnp.int32)
    near = z + 1 - 2 * (z % 2)
    far_end = 3 - end
    far_mid = 2 - right
    q_order = (far_end, far_mid, near, z)
    kv_order = (
        far_end + ends * (far_mid - far_end), far_mid + ends * (far_end - far_mid), near, z,
    )
    peers = (s + 1 - 2 * (s % 2), s + 2 - 4 * (s // 2), 3 - s)

    def kv_weights(k):
        at = pl.ds(pl.multiple_of(kv_order[k] * 256, 128), 256)
        return [
            pltpu.make_async_copy(source.at[:, at], wkv.at[k, :, i * 256 : i * 256 + 256], wkv_sem.at[k])
            for i, source in enumerate((wk_hbm, wv_hbm))
        ]

    def kv_weights_wait(k):
        pltpu.make_async_copy(wkv.at[k], wkv.at[k], wkv_sem.at[k]).wait()

    def q_weights(k):
        at = pl.ds(pl.multiple_of(q_order[k] * 1024, 128), 1024)
        return pltpu.make_async_copy(wq_hbm.at[:, at], wq.at[k], wq_sem.at[k])

    x_copy = pltpu.make_async_copy(x_hbm, x, in_sem.at[0])
    doc_copy = pltpu.make_async_copy(doc_hbm, doc, in_sem.at[1])
    x_copy.start()
    for k in range(CHIPS):
        for copy in kv_weights(k):
            copy.start()

    is_hub = z == 1
    outward = (s, 2 * near + c)

    def signal(sem, device):
        pl.semaphore_signal(sem, inc=1, device_id=device, device_id_type=MESH)

    barrier = pltpu.get_barrier_semaphore()
    signal(barrier, sibling)
    signal(barrier, outward)

    @pl.when(is_mid)
    def _():
        signal(barrier, (s, 2 * near + other))
        signal(barrier, (s, 2 * (3 - z) + c))

    @pl.when(is_hub)
    def _():
        for peer in peers:
            signal(barrier, (peer, f))

    hub = is_hub.astype(jnp.int32)
    expected = 3 + 3 * hub

    def dot(a, b):
        return jnp.dot(a, b, preferred_element_type=F32)

    def sib_copy(q, k):
        pieces = pl.ds(1, 2) if q else pl.ds(0, 1)
        return pltpu.make_async_remote_copy(
            src_ref=part.at[other, pieces, k], dst_ref=sib.at[pieces, k],
            send_sem=send_sem, recv_sem=sib_recv.at[q, k],
            device_id=sibling, device_id_type=MESH,
        )

    def raw_copy(i):
        lane = (c, other)[i]
        return pltpu.make_async_remote_copy(
            src_ref=part.at[lane, 0, 0, :, :HD], dst_ref=zin.at[0, i, :, :HD],
            send_sem=send_sem, recv_sem=raw_recv.at[i],
            device_id=(s, 2 * near + lane), device_id_type=MESH,
        )

    def first_sib_copy():
        return pltpu.make_async_remote_copy(
            src_ref=part.at[other, 0, 0, :, HD:], dst_ref=sib.at[0, 0, :, HD:],
            send_sem=send_sem, recv_sem=sib_recv.at[0, 0],
            device_id=sibling, device_id_type=MESH,
        )

    def first_z_copy():
        return pltpu.make_async_remote_copy(
            src_ref=part.at[c, 0, 0, :, HD:], dst_ref=zin.at[0, 0, :, HD:],
            send_sem=send_sem, recv_sem=arrived(0, 0, 0),
            device_id=outward, device_id_type=MESH,
        )

    def forward_first():
        first_sib_copy().wait_recv()
        part[c, 0, 0, :, HD:] = (
            part[c, 0, 0, :, HD:].astype(F32) + sib[0, 0, :, HD:].astype(F32)
        ).astype(BF)
        first_z_copy().start()

    def merge_first():
        sib_copy(0, 1).wait_recv()
        total = pair_sum(0, 1)
        for i in range(2):
            raw_copy(i).wait_recv()
        first_z_copy().wait_recv()
        part[c, 0, 1, :, :HD] = (
            total[:, :HD] + zin[0, 0, :, :HD].astype(F32) + zin[0, 1, :, :HD].astype(F32)
        ).astype(BF)
        part[c, 0, 1, :, HD:] = (total[:, HD:] + zin[0, 0, :, HD:].astype(F32)).astype(BF)
        z_copy(0, 1, 0, far_mid, 3).start()

    def project_kv(k):
        products = dot(x[...], wkv[k]).astype(BF)
        for lane in range(2):
            for i in range(2):
                at = i * WIDE + lane * HD
                part[lane, 0, k, :, i * HD : (i + 1) * HD] = products[:, at : at + HD]

    def project_queries(k):
        q_weights(k).wait()
        rows = x[...]
        for p in (1, 2):
            for lane in range(2):
                at = lane * 512 + (p - 1) * WIDE
                part[lane, p, k] = dot(rows, wq[k, :, at : at + WIDE]).astype(BF)
        sib_copy(1, k).start()

    def half(h):
        return slice(h * HALF, (h + 1) * HALF)

    def cuts(p):
        return [half(0), half(1)] if p else [slice(0, ROWS)]

    def arrived(p, slot, h):
        return z_recv.at[(max(slot - 1, 0), 3 + 2 * slot + h, 11 + 2 * slot + h)[p]]

    def z_copy(p, k, h, chip, slot):
        rows = cuts(p)[h]
        return pltpu.make_async_remote_copy(
            src_ref=part.at[c, p, k, rows], dst_ref=zin.at[p, slot, rows],
            send_sem=send_sem, recv_sem=arrived(p, slot, h),
            device_id=(s, 2 * chip + c), device_id_type=MESH,
        )

    def z_arrival(p, slot, h=0):
        z_copy(p, 0, h, near, slot).wait_recv()

    def pair_sum(p, k):
        return part[c, p, k].astype(F32) + sib[p, k].astype(F32)

    def forward(q, k, chip, slot):
        sib_copy(q, k).wait_recv()
        pieces = (1, 2) if q else (0,)
        for p in pieces:
            part[c, p, k] = pair_sum(p, k).astype(BF)
            for h in range(len(cuts(p))):
                z_copy(p, k, h, chip, slot).start()

    def merge(q, k, slot, chip):
        sib_copy(q, k).wait_recv()
        pieces = (1, 2) if q else (0,)
        for p in pieces:
            total = pair_sum(p, k)
            for h, rows in enumerate(cuts(p)):
                z_arrival(p, slot, h)
                part[c, p, k, rows] = (total[rows] + zin[p, slot, rows].astype(F32)).astype(BF)
                z_copy(p, k, h, chip, 3).start()

    def kv_copies(i):
        return [
            pltpu.make_async_remote_copy(
                src_ref=kv.at[i, s], dst_ref=kv.at[i, s],
                send_sem=send_sem, recv_sem=kv_recv.at[i],
                device_id=(peer, f), device_id_type=MESH,
            )
            for peer in peers[::-1]
        ]

    def kv_arrival(i):
        pltpu.make_async_copy(kv.at[i, pl.ds(0, 3)], kv.at[i, pl.ds(0, 3)], kv_recv.at[i]).wait()

    def share_kv():
        sib_copy(0, 3).wait_recv()
        for slot in (2, 3):
            z_arrival(0, slot)

        @pl.when(is_end)
        def _():
            z_arrival(0, 1)

        for i in range(2):
            at = slice(i * HD, (i + 1) * HD)
            total = (
                part[c, 0, 3, :, at].astype(F32) + sib[0, 3, :, at].astype(F32)
                + zin[0, 2, :, at].astype(F32) + zin[0, 3, :, at].astype(F32)
            )
            further = jnp.where(is_end, zin[0, 1, :, at].astype(F32), 0.0)
            kv[i, s] = (total + further).astype(BF)
            for copy in kv_copies(i):
                copy.start()

    def weigh(p, h):
        for slot in (3, 2):
            z_arrival(p, slot, h)
        queries = (
            part[c, p, 3, half(h)].astype(F32) + sib[p, 3, half(h)].astype(F32)
            + zin[p, 3, half(h)].astype(F32) + zin[p, 2, half(h)].astype(F32)
        ).astype(BF)
        heads = jnp.concatenate([queries[:, :HD], queries[:, HD:]], axis=0)
        keys = kv[0].reshape(STRIPES * ROWS, HD)
        scores = lax.dot_general(
            heads, keys, (((1,), (1,)), ((), ())), preferred_element_type=F32
        ) * HD ** (-0.5)
        masked = (
            scores.reshape(2, HALF, STRIPES * ROWS) + bias[half(h)][None]
        ).reshape(2 * HALF, STRIPES * ROWS)
        weights = jnp.exp(masked - jnp.max(masked, axis=1, keepdims=True))
        return weights.astype(BF), jnp.sum(weights, axis=1, keepdims=True)

    def attend(p, h, weighed):
        rounded, totals = weighed
        values = kv[1].reshape(STRIPES * ROWS, HD)
        result = (dot(rounded, values) / totals).astype(BF)
        at = (p - 1) * WIDE
        o_ref[half(h), at : at + HD] = result[:HALF]
        o_ref[half(h), at + HD : at + WIDE] = result[HALF:]

    x_copy.wait()
    kv_weights_wait(0)
    project_kv(0)
    pl.semaphore_wait(barrier, expected)

    @pl.when(is_end)
    def _():
        for i in range(2):
            raw_copy(i).start()
        first_sib_copy().start()

    @pl.when(is_mid)
    def _():
        sib_copy(0, 0).start()

    q_weights(0).start()

    @pl.when(is_mid)
    def _():
        signal(line_sem, (s, 2 * (3 - z) + c))

    for k in (1, 2, 3):
        kv_weights_wait(k)
    for k in (1, 2, 3):
        project_kv(k)
    for k in (1, 2, 3):
        sib_copy(0, k).start()
    for k in (1, 2, 3):
        q_weights(k).start()
    doc_copy.start()

    @pl.when(is_mid)
    def _():
        pl.semaphore_wait(line_sem, 1)
        signal(line_sem, outward)
        forward(0, 2, near, 2)

    @pl.when(is_end)
    def _():
        forward_first()

    @pl.when(z == 0)
    def _():
        forward(0, 2, near, 2)

    project_queries(0)

    @pl.when(z == 3)
    def _():
        pl.semaphore_wait(line_sem, 1)
        forward(0, 1, far_end, 1)
        forward(0, 2, near, 2)

    @pl.when(is_mid)
    def _():
        forward(0, 0, far_end, 3)

    @pl.when(is_hub)
    def _():
        for peer in peers:
            signal(plane_sem, (peer, f))

    project_queries(1)

    @pl.when(is_end)
    def _():
        forward(1, 0, near, 0)

    @pl.when(z == 0)
    def _():
        pl.semaphore_wait(line_sem, 1)
        forward(0, 1, far_end, 1)

    project_queries(2)
    project_queries(3)

    @pl.when(is_end)
    def _():
        forward(1, 1, near, 1)

    forward(1, 2, near, 2)

    @pl.when(is_mid)
    def _():
        merge_first()

    @pl.when(is_hub)
    def _():
        pl.semaphore_wait(plane_sem, 3)
        signal(all_sem, (s, 2 * (3 - z) + c))
        signal(all_sem, outward)

    @pl.when(z != 1)
    def _():
        pl.semaphore_wait(all_sem, 1)

    @pl.when(z == 2)
    def _():
        signal(all_sem, outward)

    share_kv()

    @pl.when(is_mid)
    def _():
        for k in range(2):
            merge(1, k, k, q_order[k])

    doc_copy.wait()
    tokens = STRIPES * ROWS
    by_pos = jnp.broadcast_to(doc[...], (8, tokens)).astype(BF)
    stored = lax.broadcasted_iota(jnp.int32, (tokens, tokens), 0)
    placed = lax.broadcasted_iota(jnp.int32, (tokens, tokens), 1)
    pick_keys = (placed == (stored & (ROWS - 1)) * STRIPES + (stored >> 7)).astype(F32).astype(BF)
    key_doc = lax.dot_general(
        by_pos, pick_keys, (((1,), (1,)), ((), ())), preferred_element_type=F32
    )[:1]
    mine = lax.broadcasted_iota(jnp.int32, (ROWS, tokens), 0) * STRIPES + s
    column = lax.broadcasted_iota(jnp.int32, (ROWS, tokens), 1)
    pick_rows = (column == mine).astype(F32).astype(BF)
    query_doc = lax.dot_general(
        pick_rows, by_pos, (((1,), (1,)), ((), ())), preferred_element_type=F32
    )[:, :1]
    key_pos = (column & (ROWS - 1)) * STRIPES + (column >> 7)
    allowed = (key_pos <= mine) & (key_doc == query_doc)
    bias[...] = jnp.where(allowed, 0.0, -1e30)

    sib_copy(1, 3).wait_recv()
    kv_arrival(0)
    early = [weigh(1, h) for h in range(2)]
    kv_arrival(1)
    for h in range(2):
        attend(1, h, early[h])
    for h in range(2):
        attend(2, h, weigh(2, h))

    pltpu.make_async_copy(part, part, send_sem).wait()


def fused(activations, query_weight, key_weight, value_weight, document_ids):
    depth = activations.shape[1]
    operands = (
        activations, document_ids.reshape(1, -1), query_weight, key_weight, value_weight,
    )
    return pl.pallas_call(
        fused_kernel,
        out_shape=jax.ShapeDtypeStruct((ROWS, 4 * HD), BF),
        in_specs=[pl.BlockSpec(memory_space=pltpu.HBM)] * 5,
        out_specs=pl.BlockSpec(memory_space=pltpu.VMEM),
        scratch_shapes=[
            pltpu.VMEM((ROWS, depth), BF),
            pltpu.VMEM((1, STRIPES * ROWS), jnp.int32),
            pltpu.VMEM((CHIPS, depth, 1024), BF),
            pltpu.VMEM((CHIPS, depth, 512), BF),
            pltpu.VMEM((2, PIECES, CHIPS, ROWS, WIDE), BF),
            pltpu.VMEM((PIECES, CHIPS, ROWS, WIDE), BF),
            pltpu.VMEM((PIECES, CHIPS, ROWS, WIDE), BF),
            pltpu.VMEM((2, STRIPES, ROWS, HD), BF),
            pltpu.VMEM((ROWS, STRIPES * ROWS), F32),
            pltpu.SemaphoreType.DMA((2,)),
            pltpu.SemaphoreType.DMA((CHIPS,)),
            pltpu.SemaphoreType.DMA((CHIPS,)),
            pltpu.SemaphoreType.DMA,
            pltpu.SemaphoreType.DMA((2, CHIPS)),
            pltpu.SemaphoreType.DMA((2,)),
            pltpu.SemaphoreType.DMA((19,)),
            pltpu.SemaphoreType.DMA((2,)),
            pltpu.SemaphoreType.REGULAR,
            pltpu.SemaphoreType.REGULAR,
            pltpu.SemaphoreType.REGULAR,
        ],
        compiler_params=pltpu.CompilerParams(
            collective_id=0, has_side_effects=True, vmem_limit_bytes=53 * 1024 * 1024
        ),
    )(*[pltpu.with_memory_space_constraint(operand, pltpu.HBM) for operand in operands])


def solution(mesh):
    small = mesh.shape["seq"] == STRIPES and mesh.shape["feat"] == 2 * CHIPS
    return jax.shard_map(
        fused if small else local,
        mesh=mesh,
        in_specs=(P("seq", "feat"), P("feat", None), P("feat", None), P("feat", None), P()),
        out_specs=P("seq", "feat"),
        check_vma=False,
    )
```

```python
import jax
import jax.numpy as jnp
from jax import lax
from jax.experimental import pallas as pl
from jax.experimental.pallas import tpu as pltpu
from jax.sharding import PartitionSpec as P

H = 32
KVH = 8
HD = 128


def passed_along(value, axis, steps):
    count = lax.axis_size(axis)
    pairs = [(source, (source + steps) % count) for source in range(count)]
    return lax.ppermute(value, axis, pairs)


def attend_block(
    softmax_state, kv_block, source, query_heads, query_pos, query_doc, doc_table, stripes
):
    maxima, totals, accumulated = softmax_state
    row_count = kv_block.shape[0]
    head_size = kv_block.shape[1] // 2
    key_rows = kv_block[:, :head_size]
    value_rows = kv_block[:, head_size:]
    key_pos = jnp.arange(row_count, dtype=jnp.int32) * stripes + source
    key_doc = lax.dynamic_slice_in_dim(doc_table, source, 1, 1)[:, 0]
    allowed = (key_pos[None, :] <= query_pos[:, None]) & (key_doc[None, :] == query_doc[:, None])
    scores = jnp.einsum(
        "qhd,kd->hqk", query_heads, key_rows, preferred_element_type=jnp.float32
    ) * head_size ** (-0.5)
    masked = jnp.where(allowed[None], scores, -1e30)
    newmax = jnp.maximum(maxima, jnp.max(masked, axis=2))
    weights = jnp.where(allowed[None], jnp.exp(scores - newmax[..., None]), 0.0)
    factor = jnp.exp(maxima - newmax)
    totals = totals * factor + jnp.sum(weights, axis=2)
    accumulated = accumulated * factor[..., None] + jnp.einsum(
        "hqk,kd->hqd", weights.astype(jnp.bfloat16), value_rows, preferred_element_type=jnp.float32
    )
    return (newmax, totals, accumulated)


def local(activations, query_weight, key_weight, value_weight, document_ids):
    row_count = activations.shape[0]
    features = lax.axis_size("feat")
    stripes = lax.axis_size("seq")
    seq_rank = lax.axis_index("seq")
    per_device = H // features
    group_size = H // KVH
    query_part = jnp.dot(activations, query_weight, preferred_element_type=jnp.float32).astype(
        jnp.bfloat16
    )
    key_part = jnp.dot(activations, key_weight, preferred_element_type=jnp.float32).astype(
        jnp.bfloat16
    )
    value_part = jnp.dot(activations, value_weight, preferred_element_type=jnp.float32).astype(
        jnp.bfloat16
    )
    owners = [rank * per_device // group_size for rank in range(features)]

    def by_owner(part):
        return jnp.stack([part[:, owner * HD : (owner + 1) * HD] for owner in owners], axis=1)

    stacked = jnp.concatenate(
        [
            query_part.reshape(row_count, features, per_device * HD),
            by_owner(key_part),
            by_owner(value_part),
        ],
        axis=2,
    ).reshape(row_count, features * (per_device + 2) * HD)
    summed = (
        lax.psum_scatter(stacked, "feat", scatter_dimension=1, tiled=True)
        .astype(jnp.float32)
        .astype(jnp.bfloat16)
    )
    queries = summed[:, : per_device * HD]
    kv_block = summed[:, per_device * HD :]
    query_heads = queries.reshape(row_count, per_device, HD)
    query_pos = jnp.arange(row_count, dtype=jnp.int32) * stripes + seq_rank
    doc_table = document_ids.reshape(row_count, stripes)
    query_doc = lax.dynamic_slice_in_dim(doc_table, seq_rank, 1, 1)[:, 0]

    def visit_block(running, current, source):
        return attend_block(
            running, current, source, query_heads, query_pos, query_doc, doc_table, stripes
        )

    softmax_state = (
        jnp.full((per_device, row_count), -1e30, jnp.float32),
        jnp.zeros((per_device, row_count), jnp.float32),
        jnp.zeros((per_device, row_count, HD), jnp.float32),
    )
    softmax_state = visit_block(softmax_state, kv_block, seq_rank)

    def advance(cycle_step, loop_carry):
        current, running = loop_carry
        current = passed_along(current, "seq", 1)
        return (current, visit_block(running, current, (seq_rank - cycle_step) % stripes))

    loop_carry = lax.fori_loop(1, stripes, advance, (kv_block, softmax_state))
    softmax_state = loop_carry[1]
    maxima, totals, accumulated = softmax_state
    output = (accumulated / totals[..., None]).astype(jnp.bfloat16)
    return output.transpose(1, 0, 2).reshape(row_count, per_device * HD)


MESH = pl.DeviceIdType.MESH
ROWS = 128
HALF = 64
WIDE = 256
PIECES = 3
CHIPS = 4
STRIPES = 4
BF = jnp.bfloat16
F32 = jnp.float32


def fused_kernel(
    x_hbm, doc_hbm, wq_hbm, wk_hbm, wv_hbm, o_ref,
    x, doc, wq, wkv, part, sib, zin, kv, bias,
    in_sem, wkv_sem, wq_sem, send_sem, sib_recv, raw_recv, z_recv, kv_recv,
    line_sem, plane_sem, all_sem,
):
    s = lax.axis_index("seq")
    f = lax.axis_index("feat")
    z = f // 2
    c = f % 2
    other = 1 - c
    sibling = (s, f + 1 - 2 * c)
    right = z // 2
    end = 3 * right
    is_end = z == end
    is_mid = z != end
    ends = is_end.astype(jnp.int32)
    near = z + 1 - 2 * (z % 2)
    far_end = 3 - end
    far_mid = 2 - right
    q_order = (far_end, far_mid, near, z)
    kv_order = (
        far_end + ends * (far_mid - far_end), far_mid + ends * (far_end - far_mid), near, z,
    )
    peers = (s + 1 - 2 * (s % 2), s + 2 - 4 * (s // 2), 3 - s)

    def kv_weights(k):
        at = pl.ds(pl.multiple_of(kv_order[k] * 256, 128), 256)
        return [
            pltpu.make_async_copy(source.at[:, at], wkv.at[k, :, i * 256 : i * 256 + 256], wkv_sem.at[k])
            for i, source in enumerate((wk_hbm, wv_hbm))
        ]

    def kv_weights_wait(k):
        pltpu.make_async_copy(wkv.at[k], wkv.at[k], wkv_sem.at[k]).wait()

    def q_weights(k):
        at = pl.ds(pl.multiple_of(q_order[k] * 1024, 128), 1024)
        return pltpu.make_async_copy(wq_hbm.at[:, at], wq.at[k], wq_sem.at[k])

    x_copy = pltpu.make_async_copy(x_hbm, x, in_sem.at[0])
    doc_copy = pltpu.make_async_copy(doc_hbm, doc, in_sem.at[1])
    x_copy.start()
    for k in range(CHIPS):
        for copy in kv_weights(k):
            copy.start()

    is_hub = z == 0
    outward = (s, 2 * near + c)

    def signal(sem, device):
        pl.semaphore_signal(sem, inc=1, device_id=device, device_id_type=MESH)

    barrier = pltpu.get_barrier_semaphore()
    signal(barrier, sibling)
    signal(barrier, outward)

    @pl.when(is_mid)
    def _():
        signal(barrier, (s, 2 * near + other))
        signal(barrier, (s, 2 * (3 - z) + c))

    @pl.when(is_hub)
    def _():
        for peer in peers:
            signal(barrier, (peer, f))

    hub = is_hub.astype(jnp.int32)
    expected = 3 + 3 * hub

    def dot(a, b):
        return jnp.dot(a, b, preferred_element_type=F32)

    def sib_copy(q, k):
        pieces = pl.ds(1, 2) if q else pl.ds(0, 1)
        return pltpu.make_async_remote_copy(
            src_ref=part.at[other, pieces, k], dst_ref=sib.at[pieces, k],
            send_sem=send_sem, recv_sem=sib_recv.at[q, k],
            device_id=sibling, device_id_type=MESH,
        )

    def raw_copy(i):
        lane = (c, other)[i]
        return pltpu.make_async_remote_copy(
            src_ref=part.at[lane, 0, 0, :, :HD], dst_ref=zin.at[0, i, :, :HD],
            send_sem=send_sem, recv_sem=raw_recv.at[i],
            device_id=(s, 2 * near + lane), device_id_type=MESH,
        )

    def first_sib_copy():
        return pltpu.make_async_remote_copy(
            src_ref=part.at[other, 0, 0, :, HD:], dst_ref=sib.at[0, 0, :, HD:],
            send_sem=send_sem, recv_sem=sib_recv.at[0, 0],
            device_id=sibling, device_id_type=MESH,
        )

    def first_z_copy():
        return pltpu.make_async_remote_copy(
            src_ref=part.at[c, 0, 0, :, HD:], dst_ref=zin.at[0, 0, :, HD:],
            send_sem=send_sem, recv_sem=arrived(0, 0, 0),
            device_id=outward, device_id_type=MESH,
        )

    def forward_first():
        first_sib_copy().wait_recv()
        part[c, 0, 0, :, HD:] = (
            part[c, 0, 0, :, HD:].astype(F32) + sib[0, 0, :, HD:].astype(F32)
        ).astype(BF)
        first_z_copy().start()

    def merge_first():
        sib_copy(0, 1).wait_recv()
        total = pair_sum(0, 1)
        for i in range(2):
            raw_copy(i).wait_recv()
        first_z_copy().wait_recv()
        part[c, 0, 1, :, :HD] = (
            total[:, :HD] + zin[0, 0, :, :HD].astype(F32) + zin[0, 1, :, :HD].astype(F32)
        ).astype(BF)
        part[c, 0, 1, :, HD:] = (total[:, HD:] + zin[0, 0, :, HD:].astype(F32)).astype(BF)
        z_copy(0, 1, 0, far_mid, 3).start()

    def project_kv(k):
        products = dot(x[...], wkv[k]).astype(BF)
        for lane in range(2):
            for i in range(2):
                at = i * WIDE + lane * HD
                part[lane, 0, k, :, i * HD : (i + 1) * HD] = products[:, at : at + HD]

    def project_queries(k):
        q_weights(k).wait()
        rows = x[...]
        for p in (1, 2):
            for lane in range(2):
                at = lane * 512 + (p - 1) * WIDE
                part[lane, p, k] = dot(rows, wq[k, :, at : at + WIDE]).astype(BF)
        sib_copy(1, k).start()

    def half(h):
        return slice(h * HALF, (h + 1) * HALF)

    def cuts(p):
        return [half(0), half(1)] if p else [slice(0, ROWS)]

    def arrived(p, slot, h):
        return z_recv.at[(max(slot - 1, 0), 3 + 2 * slot + h, 11 + 2 * slot + h)[p]]

    def z_copy(p, k, h, chip, slot):
        rows = cuts(p)[h]
        return pltpu.make_async_remote_copy(
            src_ref=part.at[c, p, k, rows], dst_ref=zin.at[p, slot, rows],
            send_sem=send_sem, recv_sem=arrived(p, slot, h),
            device_id=(s, 2 * chip + c), device_id_type=MESH,
        )

    def z_arrival(p, slot, h=0):
        z_copy(p, 0, h, near, slot).wait_recv()

    def pair_sum(p, k):
        return part[c, p, k].astype(F32) + sib[p, k].astype(F32)

    def forward(q, k, chip, slot):
        sib_copy(q, k).wait_recv()
        pieces = (1, 2) if q else (0,)
        for p in pieces:
            part[c, p, k] = pair_sum(p, k).astype(BF)
            for h in range(len(cuts(p))):
                z_copy(p, k, h, chip, slot).start()

    def merge(q, k, slot, chip):
        sib_copy(q, k).wait_recv()
        pieces = (1, 2) if q else (0,)
        for p in pieces:
            total = pair_sum(p, k)
            for h, rows in enumerate(cuts(p)):
                z_arrival(p, slot, h)
                part[c, p, k, rows] = (total[rows] + zin[p, slot, rows].astype(F32)).astype(BF)
                z_copy(p, k, h, chip, 3).start()

    def kv_copies(i):
        return [
            pltpu.make_async_remote_copy(
                src_ref=kv.at[i, s], dst_ref=kv.at[i, s],
                send_sem=send_sem, recv_sem=kv_recv.at[i],
                device_id=(peer, f), device_id_type=MESH,
            )
            for peer in peers[::-1]
        ]

    def kv_arrival(i):
        pltpu.make_async_copy(kv.at[i, pl.ds(0, 3)], kv.at[i, pl.ds(0, 3)], kv_recv.at[i]).wait()

    def share_kv():
        sib_copy(0, 3).wait_recv()
        for slot in (2, 3):
            z_arrival(0, slot)

        @pl.when(is_end)
        def _():
            z_arrival(0, 1)

        for i in range(2):
            at = slice(i * HD, (i + 1) * HD)
            total = (
                part[c, 0, 3, :, at].astype(F32) + sib[0, 3, :, at].astype(F32)
                + zin[0, 2, :, at].astype(F32) + zin[0, 3, :, at].astype(F32)
            )
            further = jnp.where(is_end, zin[0, 1, :, at].astype(F32), 0.0)
            kv[i, s] = (total + further).astype(BF)
            for copy in kv_copies(i):
                copy.start()

    def weigh(p, h):
        for slot in (3, 2):
            z_arrival(p, slot, h)
        queries = (
            part[c, p, 3, half(h)].astype(F32) + sib[p, 3, half(h)].astype(F32)
            + zin[p, 3, half(h)].astype(F32) + zin[p, 2, half(h)].astype(F32)
        ).astype(BF)
        heads = jnp.concatenate([queries[:, :HD], queries[:, HD:]], axis=0)
        keys = kv[0].reshape(STRIPES * ROWS, HD)
        scores = lax.dot_general(
            heads, keys, (((1,), (1,)), ((), ())), preferred_element_type=F32
        ) * HD ** (-0.5)
        masked = (
            scores.reshape(2, HALF, STRIPES * ROWS) + bias[half(h)][None]
        ).reshape(2 * HALF, STRIPES * ROWS)
        weights = jnp.exp(masked - jnp.max(masked, axis=1, keepdims=True))
        return weights.astype(BF), jnp.sum(weights, axis=1, keepdims=True)

    def attend(p, h, weighed):
        rounded, totals = weighed
        values = kv[1].reshape(STRIPES * ROWS, HD)
        result = (dot(rounded, values) / totals).astype(BF)
        at = (p - 1) * WIDE
        o_ref[half(h), at : at + HD] = result[:HALF]
        o_ref[half(h), at + HD : at + WIDE] = result[HALF:]

    x_copy.wait()
    kv_weights_wait(0)
    project_kv(0)
    pl.semaphore_wait(barrier, expected)

    @pl.when(is_end)
    def _():
        for i in range(2):
            raw_copy(i).start()
        first_sib_copy().start()

    @pl.when(is_mid)
    def _():
        sib_copy(0, 0).start()

    q_weights(0).start()

    @pl.when(is_mid)
    def _():
        signal(line_sem, (s, 2 * (3 - z) + c))

    for k in (1, 2, 3):
        kv_weights_wait(k)
    for k in (1, 2, 3):
        project_kv(k)
    for k in (1, 2, 3):
        sib_copy(0, k).start()
    for k in (1, 2, 3):
        q_weights(k).start()
    doc_copy.start()

    @pl.when(is_mid)
    def _():
        pl.semaphore_wait(line_sem, 1)
        signal(line_sem, outward)
        forward(0, 2, near, 2)

    @pl.when(is_end)
    def _():
        forward_first()

    @pl.when(z == 0)
    def _():
        forward(0, 2, near, 2)

    project_queries(0)

    @pl.when(z == 3)
    def _():
        pl.semaphore_wait(line_sem, 1)
        forward(0, 1, far_end, 1)
        forward(0, 2, near, 2)

    @pl.when(is_mid)
    def _():
        forward(0, 0, far_end, 3)

    project_queries(1)

    @pl.when(is_end)
    def _():
        forward(1, 0, near, 0)

    @pl.when(z == 0)
    def _():
        pl.semaphore_wait(line_sem, 1)
        for peer in peers:
            signal(plane_sem, (peer, f))
        forward(0, 1, far_end, 1)

    project_queries(2)
    project_queries(3)

    @pl.when(is_end)
    def _():
        forward(1, 1, near, 1)

    forward(1, 2, near, 2)

    @pl.when(is_mid)
    def _():
        merge_first()

    @pl.when(is_hub)
    def _():
        pl.semaphore_wait(plane_sem, 3)
        signal(all_sem, outward)

    @pl.when(z != 0)
    def _():
        pl.semaphore_wait(all_sem, 1)

    @pl.when(z == 1)
    def _():
        signal(all_sem, (s, 2 * (3 - z) + c))

    @pl.when(z == 2)
    def _():
        signal(all_sem, outward)

    share_kv()

    @pl.when(is_mid)
    def _():
        for k in range(2):
            merge(1, k, k, q_order[k])

    doc_copy.wait()
    tokens = STRIPES * ROWS
    by_pos = jnp.broadcast_to(doc[...], (8, tokens)).astype(BF)
    stored = lax.broadcasted_iota(jnp.int32, (tokens, tokens), 0)
    placed = lax.broadcasted_iota(jnp.int32, (tokens, tokens), 1)
    pick_keys = (placed == (stored & (ROWS - 1)) * STRIPES + (stored >> 7)).astype(F32).astype(BF)
    key_doc = lax.dot_general(
        by_pos, pick_keys, (((1,), (1,)), ((), ())), preferred_element_type=F32
    )[:1]
    mine = lax.broadcasted_iota(jnp.int32, (ROWS, tokens), 0) * STRIPES + s
    column = lax.broadcasted_iota(jnp.int32, (ROWS, tokens), 1)
    pick_rows = (column == mine).astype(F32).astype(BF)
    query_doc = lax.dot_general(
        pick_rows, by_pos, (((1,), (1,)), ((), ())), preferred_element_type=F32
    )[:, :1]
    key_pos = (column & (ROWS - 1)) * STRIPES + (column >> 7)
    allowed = (key_pos <= mine) & (key_doc == query_doc)
    bias[...] = jnp.where(allowed, 0.0, -1e30)

    sib_copy(1, 3).wait_recv()
    kv_arrival(0)
    early = [weigh(1, h) for h in range(2)]
    kv_arrival(1)
    for h in range(2):
        attend(1, h, early[h])
    for h in range(2):
        attend(2, h, weigh(2, h))

    pltpu.make_async_copy(part, part, send_sem).wait()


def fused(activations, query_weight, key_weight, value_weight, document_ids):
    depth = activations.shape[1]
    operands = (
        activations, document_ids.reshape(1, -1), query_weight, key_weight, value_weight,
    )
    return pl.pallas_call(
        fused_kernel,
        out_shape=jax.ShapeDtypeStruct((ROWS, 4 * HD), BF),
        in_specs=[pl.BlockSpec(memory_space=pltpu.HBM)] * 5,
        out_specs=pl.BlockSpec(memory_space=pltpu.VMEM),
        scratch_shapes=[
            pltpu.VMEM((ROWS, depth), BF),
            pltpu.VMEM((1, STRIPES * ROWS), jnp.int32),
            pltpu.VMEM((CHIPS, depth, 1024), BF),
            pltpu.VMEM((CHIPS, depth, 512), BF),
            pltpu.VMEM((2, PIECES, CHIPS, ROWS, WIDE), BF),
            pltpu.VMEM((PIECES, CHIPS, ROWS, WIDE), BF),
            pltpu.VMEM((PIECES, CHIPS, ROWS, WIDE), BF),
            pltpu.VMEM((2, STRIPES, ROWS, HD), BF),
            pltpu.VMEM((ROWS, STRIPES * ROWS), F32),
            pltpu.SemaphoreType.DMA((2,)),
            pltpu.SemaphoreType.DMA((CHIPS,)),
            pltpu.SemaphoreType.DMA((CHIPS,)),
            pltpu.SemaphoreType.DMA,
            pltpu.SemaphoreType.DMA((2, CHIPS)),
            pltpu.SemaphoreType.DMA((2,)),
            pltpu.SemaphoreType.DMA((19,)),
            pltpu.SemaphoreType.DMA((2,)),
            pltpu.SemaphoreType.REGULAR,
            pltpu.SemaphoreType.REGULAR,
            pltpu.SemaphoreType.REGULAR,
        ],
        compiler_params=pltpu.CompilerParams(
            collective_id=0, has_side_effects=True, vmem_limit_bytes=53 * 1024 * 1024
        ),
    )(*[pltpu.with_memory_space_constraint(operand, pltpu.HBM) for operand in operands])


def solution(mesh):
    small = mesh.shape["seq"] == STRIPES and mesh.shape["feat"] == 2 * CHIPS
    return jax.shard_map(
        fused if small else local,
        mesh=mesh,
        in_specs=(P("seq", "feat"), P("feat", None), P("feat", None), P("feat", None), P()),
        out_specs=P("seq", "feat"),
        check_vma=False,
    )
```

```python
import jax
import jax.numpy as jnp
from jax import lax
from jax.experimental import pallas as pl
from jax.experimental.pallas import tpu as pltpu
from jax.sharding import PartitionSpec as P

H = 32
KVH = 8
HD = 128


def passed_along(value, axis, steps):
    count = lax.axis_size(axis)
    pairs = [(source, (source + steps) % count) for source in range(count)]
    return lax.ppermute(value, axis, pairs)


def attend_block(
    softmax_state, kv_block, source, query_heads, query_pos, query_doc, doc_table, stripes
):
    maxima, totals, accumulated = softmax_state
    row_count = kv_block.shape[0]
    head_size = kv_block.shape[1] // 2
    key_rows = kv_block[:, :head_size]
    value_rows = kv_block[:, head_size:]
    key_pos = jnp.arange(row_count, dtype=jnp.int32) * stripes + source
    key_doc = lax.dynamic_slice_in_dim(doc_table, source, 1, 1)[:, 0]
    allowed = (key_pos[None, :] <= query_pos[:, None]) & (key_doc[None, :] == query_doc[:, None])
    scores = jnp.einsum(
        "qhd,kd->hqk", query_heads, key_rows, preferred_element_type=jnp.float32
    ) * head_size ** (-0.5)
    masked = jnp.where(allowed[None], scores, -1e30)
    newmax = jnp.maximum(maxima, jnp.max(masked, axis=2))
    weights = jnp.where(allowed[None], jnp.exp(scores - newmax[..., None]), 0.0)
    factor = jnp.exp(maxima - newmax)
    totals = totals * factor + jnp.sum(weights, axis=2)
    accumulated = accumulated * factor[..., None] + jnp.einsum(
        "hqk,kd->hqd", weights.astype(jnp.bfloat16), value_rows, preferred_element_type=jnp.float32
    )
    return (newmax, totals, accumulated)


def local(activations, query_weight, key_weight, value_weight, document_ids):
    row_count = activations.shape[0]
    features = lax.axis_size("feat")
    stripes = lax.axis_size("seq")
    seq_rank = lax.axis_index("seq")
    per_device = H // features
    group_size = H // KVH
    query_part = jnp.dot(activations, query_weight, preferred_element_type=jnp.float32).astype(
        jnp.bfloat16
    )
    key_part = jnp.dot(activations, key_weight, preferred_element_type=jnp.float32).astype(
        jnp.bfloat16
    )
    value_part = jnp.dot(activations, value_weight, preferred_element_type=jnp.float32).astype(
        jnp.bfloat16
    )
    owners = [rank * per_device // group_size for rank in range(features)]

    def by_owner(part):
        return jnp.stack([part[:, owner * HD : (owner + 1) * HD] for owner in owners], axis=1)

    stacked = jnp.concatenate(
        [
            query_part.reshape(row_count, features, per_device * HD),
            by_owner(key_part),
            by_owner(value_part),
        ],
        axis=2,
    ).reshape(row_count, features * (per_device + 2) * HD)
    summed = (
        lax.psum_scatter(stacked, "feat", scatter_dimension=1, tiled=True)
        .astype(jnp.float32)
        .astype(jnp.bfloat16)
    )
    queries = summed[:, : per_device * HD]
    kv_block = summed[:, per_device * HD :]
    query_heads = queries.reshape(row_count, per_device, HD)
    query_pos = jnp.arange(row_count, dtype=jnp.int32) * stripes + seq_rank
    doc_table = document_ids.reshape(row_count, stripes)
    query_doc = lax.dynamic_slice_in_dim(doc_table, seq_rank, 1, 1)[:, 0]

    def visit_block(running, current, source):
        return attend_block(
            running, current, source, query_heads, query_pos, query_doc, doc_table, stripes
        )

    softmax_state = (
        jnp.full((per_device, row_count), -1e30, jnp.float32),
        jnp.zeros((per_device, row_count), jnp.float32),
        jnp.zeros((per_device, row_count, HD), jnp.float32),
    )
    softmax_state = visit_block(softmax_state, kv_block, seq_rank)

    def advance(cycle_step, loop_carry):
        current, running = loop_carry
        current = passed_along(current, "seq", 1)
        return (current, visit_block(running, current, (seq_rank - cycle_step) % stripes))

    loop_carry = lax.fori_loop(1, stripes, advance, (kv_block, softmax_state))
    softmax_state = loop_carry[1]
    maxima, totals, accumulated = softmax_state
    output = (accumulated / totals[..., None]).astype(jnp.bfloat16)
    return output.transpose(1, 0, 2).reshape(row_count, per_device * HD)


MESH = pl.DeviceIdType.MESH
ROWS = 128
HALF = 64
WIDE = 256
PIECES = 3
CHIPS = 4
STRIPES = 4
BF = jnp.bfloat16
F32 = jnp.float32


def fused_kernel(
    x_hbm, doc_hbm, wq_hbm, wk_hbm, wv_hbm, o_ref,
    x, doc, wq, wkv, part, sib, zin, kv, bias,
    in_sem, wkv_sem, wq_sem, send_sem, sib_recv, raw_recv, z_recv, kv_recv,
    line_sem, plane_sem, all_sem,
):
    s = lax.axis_index("seq")
    f = lax.axis_index("feat")
    z = f // 2
    c = f % 2
    other = 1 - c
    sibling = (s, f + 1 - 2 * c)
    right = z // 2
    end = 3 * right
    is_end = z == end
    is_mid = z != end
    ends = is_end.astype(jnp.int32)
    near = z + 1 - 2 * (z % 2)
    far_end = 3 - end
    far_mid = 2 - right
    q_order = (far_end, far_mid, near, z)
    kv_order = (
        far_end + ends * (far_mid - far_end), far_mid + ends * (far_end - far_mid), near, z,
    )
    peers = (s + 1 - 2 * (s % 2), s + 2 - 4 * (s // 2), 3 - s)

    def kv_weights(k):
        at = pl.ds(pl.multiple_of(kv_order[k] * 256, 128), 256)
        return [
            pltpu.make_async_copy(source.at[:, at], wkv.at[k, :, i * 256 : i * 256 + 256], wkv_sem.at[min(k, 1)])
            for i, source in enumerate((wk_hbm, wv_hbm))
        ]

    def kv_weights_wait(first, count):
        held = wkv.at[pl.ds(first, count)]
        pltpu.make_async_copy(held, held, wkv_sem.at[min(first, 1)]).wait()

    def q_weights(k):
        at = pl.ds(pl.multiple_of(q_order[k] * 1024, 128), 1024)
        return pltpu.make_async_copy(wq_hbm.at[:, at], wq.at[k], wq_sem.at[k])

    x_copy = pltpu.make_async_copy(x_hbm, x, in_sem.at[0])
    doc_copy = pltpu.make_async_copy(doc_hbm, doc, in_sem.at[1])
    x_copy.start()
    for k in range(CHIPS):
        for copy in kv_weights(k):
            copy.start()

    is_hub = z == 1
    outward = (s, 2 * near + c)

    def signal(sem, device):
        pl.semaphore_signal(sem, inc=1, device_id=device, device_id_type=MESH)

    barrier = pltpu.get_barrier_semaphore()
    signal(barrier, sibling)
    signal(barrier, outward)

    @pl.when(is_mid)
    def _():
        signal(barrier, (s, 2 * near + other))
        signal(barrier, (s, 2 * (3 - z) + c))

    @pl.when(is_hub)
    def _():
        for peer in peers:
            signal(barrier, (peer, f))

    hub = is_hub.astype(jnp.int32)
    expected = 3 + 3 * hub

    def dot(a, b):
        return jnp.dot(a, b, preferred_element_type=F32)

    def sib_copy(q, k):
        pieces = pl.ds(1, 2) if q else pl.ds(0, 1)
        return pltpu.make_async_remote_copy(
            src_ref=part.at[other, pieces, k], dst_ref=sib.at[pieces, k],
            send_sem=send_sem, recv_sem=sib_recv.at[q, k],
            device_id=sibling, device_id_type=MESH,
        )

    def raw_copy(i):
        lane = (c, other)[i]
        return pltpu.make_async_remote_copy(
            src_ref=part.at[lane, 0, 0, :, :HD], dst_ref=zin.at[0, i, :, :HD],
            send_sem=send_sem, recv_sem=raw_recv.at[i],
            device_id=(s, 2 * near + lane), device_id_type=MESH,
        )

    def first_sib_copy():
        return pltpu.make_async_remote_copy(
            src_ref=part.at[other, 0, 0, :, HD:], dst_ref=sib.at[0, 0, :, HD:],
            send_sem=send_sem, recv_sem=sib_recv.at[0, 0],
            device_id=sibling, device_id_type=MESH,
        )

    def first_z_copy():
        return pltpu.make_async_remote_copy(
            src_ref=part.at[c, 0, 0, :, HD:], dst_ref=zin.at[0, 0, :, HD:],
            send_sem=send_sem, recv_sem=arrived(0, 0, 0),
            device_id=outward, device_id_type=MESH,
        )

    def forward_first():
        first_sib_copy().wait_recv()
        part[c, 0, 0, :, HD:] = (
            part[c, 0, 0, :, HD:].astype(F32) + sib[0, 0, :, HD:].astype(F32)
        ).astype(BF)
        first_z_copy().start()

    def merge_first():
        sib_copy(0, 1).wait_recv()
        total = pair_sum(0, 1)
        for i in range(2):
            raw_copy(i).wait_recv()
        first_z_copy().wait_recv()
        part[c, 0, 1, :, :HD] = (
            total[:, :HD] + zin[0, 0, :, :HD].astype(F32) + zin[0, 1, :, :HD].astype(F32)
        ).astype(BF)
        part[c, 0, 1, :, HD:] = (total[:, HD:] + zin[0, 0, :, HD:].astype(F32)).astype(BF)
        z_copy(0, 1, 0, far_mid, 3).start()

    def project_kv(k):
        products = dot(x[...], wkv[k]).astype(BF)
        for lane in range(2):
            for i in range(2):
                at = i * WIDE + lane * HD
                part[lane, 0, k, :, i * HD : (i + 1) * HD] = products[:, at : at + HD]

    def project_queries(k):
        q_weights(k).wait()
        rows = x[...]
        for p in (1, 2):
            for lane in range(2):
                at = lane * 512 + (p - 1) * WIDE
                part[lane, p, k] = dot(rows, wq[k, :, at : at + WIDE]).astype(BF)
        sib_copy(1, k).start()

    def half(h):
        return slice(h * HALF, (h + 1) * HALF)

    def cuts(p):
        return [half(0), half(1)] if p else [slice(0, ROWS)]

    def arrived(p, slot, h):
        return z_recv.at[(max(slot - 1, 0), 3 + 2 * slot + h, 11 + 2 * slot + h)[p]]

    def z_copy(p, k, h, chip, slot):
        rows = cuts(p)[h]
        return pltpu.make_async_remote_copy(
            src_ref=part.at[c, p, k, rows], dst_ref=zin.at[p, slot, rows],
            send_sem=send_sem, recv_sem=arrived(p, slot, h),
            device_id=(s, 2 * chip + c), device_id_type=MESH,
        )

    def z_arrival(p, slot, h=0):
        z_copy(p, 0, h, near, slot).wait_recv()

    def pair_sum(p, k):
        return part[c, p, k].astype(F32) + sib[p, k].astype(F32)

    def forward(q, k, chip, slot):
        sib_copy(q, k).wait_recv()
        pieces = (1, 2) if q else (0,)
        for p in pieces:
            part[c, p, k] = pair_sum(p, k).astype(BF)
            for h in range(len(cuts(p))):
                z_copy(p, k, h, chip, slot).start()

    def merge(q, k, slot, chip):
        sib_copy(q, k).wait_recv()
        pieces = (1, 2) if q else (0,)
        for p in pieces:
            total = pair_sum(p, k)
            for h, rows in enumerate(cuts(p)):
                z_arrival(p, slot, h)
                part[c, p, k, rows] = (total[rows] + zin[p, slot, rows].astype(F32)).astype(BF)
                z_copy(p, k, h, chip, 3).start()

    def kv_copies(i):
        return [
            pltpu.make_async_remote_copy(
                src_ref=kv.at[i, s], dst_ref=kv.at[i, s],
                send_sem=send_sem, recv_sem=kv_recv.at[i],
                device_id=(peer, f), device_id_type=MESH,
            )
            for peer in peers[::-1]
        ]

    def kv_arrival(i):
        pltpu.make_async_copy(kv.at[i, pl.ds(0, 3)], kv.at[i, pl.ds(0, 3)], kv_recv.at[i]).wait()

    def share_kv():
        sib_copy(0, 3).wait_recv()
        for slot in (2, 3):
            z_arrival(0, slot)

        @pl.when(is_end)
        def _():
            z_arrival(0, 1)

        for i in range(2):
            at = slice(i * HD, (i + 1) * HD)
            total = (
                part[c, 0, 3, :, at].astype(F32) + sib[0, 3, :, at].astype(F32)
                + zin[0, 2, :, at].astype(F32) + zin[0, 3, :, at].astype(F32)
            )
            further = jnp.where(is_end, zin[0, 1, :, at].astype(F32), 0.0)
            kv[i, s] = (total + further).astype(BF)
            for copy in kv_copies(i):
                copy.start()

    def weigh(p, h):
        for slot in (3, 2):
            z_arrival(p, slot, h)
        queries = (
            part[c, p, 3, half(h)].astype(F32) + sib[p, 3, half(h)].astype(F32)
            + zin[p, 3, half(h)].astype(F32) + zin[p, 2, half(h)].astype(F32)
        ).astype(BF)
        heads = jnp.concatenate([queries[:, :HD], queries[:, HD:]], axis=0)
        keys = kv[0].reshape(STRIPES * ROWS, HD)
        scores = lax.dot_general(
            heads, keys, (((1,), (1,)), ((), ())), preferred_element_type=F32
        ) * HD ** (-0.5)
        masked = (
            scores.reshape(2, HALF, STRIPES * ROWS) + bias[half(h)][None]
        ).reshape(2 * HALF, STRIPES * ROWS)
        weights = jnp.exp(masked - jnp.max(masked, axis=1, keepdims=True))
        return weights.astype(BF), jnp.sum(weights, axis=1, keepdims=True)

    def attend(p, h, weighed):
        rounded, totals = weighed
        values = kv[1].reshape(STRIPES * ROWS, HD)
        result = (dot(rounded, values) / totals).astype(BF)
        at = (p - 1) * WIDE
        o_ref[half(h), at : at + HD] = result[:HALF]
        o_ref[half(h), at + HD : at + WIDE] = result[HALF:]

    x_copy.wait()
    kv_weights_wait(0, 1)
    project_kv(0)
    pl.semaphore_wait(barrier, expected)

    @pl.when(is_end)
    def _():
        for i in range(2):
            raw_copy(i).start()
        first_sib_copy().start()

    @pl.when(is_mid)
    def _():
        sib_copy(0, 0).start()

    q_weights(0).start()

    @pl.when(is_mid)
    def _():
        signal(line_sem, (s, 2 * (3 - z) + c))

    kv_weights_wait(1, 3)
    for k in (1, 2, 3):
        project_kv(k)
    for k in (1, 2, 3):
        sib_copy(0, k).start()
    for k in (1, 2, 3):
        q_weights(k).start()
    doc_copy.start()

    @pl.when(is_mid)
    def _():
        pl.semaphore_wait(line_sem, 1)
        signal(line_sem, outward)
        forward(0, 2, near, 2)

    @pl.when(is_end)
    def _():
        forward_first()

    @pl.when(z == 0)
    def _():
        forward(0, 2, near, 2)

    project_queries(0)

    @pl.when(z == 3)
    def _():
        pl.semaphore_wait(line_sem, 1)
        forward(0, 1, far_end, 1)
        forward(0, 2, near, 2)

    @pl.when(is_mid)
    def _():
        forward(0, 0, far_end, 3)

    @pl.when(is_hub)
    def _():
        for peer in peers:
            signal(plane_sem, (peer, f))

    project_queries(1)

    @pl.when(is_end)
    def _():
        forward(1, 0, near, 0)

    @pl.when(z == 0)
    def _():
        pl.semaphore_wait(line_sem, 1)
        forward(0, 1, far_end, 1)

    project_queries(2)
    project_queries(3)

    @pl.when(is_end)
    def _():
        forward(1, 1, near, 1)

    forward(1, 2, near, 2)

    @pl.when(is_mid)
    def _():
        merge_first()

    @pl.when(is_hub)
    def _():
        pl.semaphore_wait(plane_sem, 3)
        signal(all_sem, (s, 2 * (3 - z) + c))
        signal(all_sem, outward)

    @pl.when(z != 1)
    def _():
        pl.semaphore_wait(all_sem, 1)

    @pl.when(z == 2)
    def _():
        signal(all_sem, outward)

    share_kv()

    @pl.when(is_mid)
    def _():
        for k in range(2):
            merge(1, k, k, q_order[k])

    doc_copy.wait()
    tokens = STRIPES * ROWS
    by_pos = jnp.broadcast_to(doc[...], (8, tokens)).astype(BF)
    stored = lax.broadcasted_iota(jnp.int32, (tokens, tokens), 0)
    placed = lax.broadcasted_iota(jnp.int32, (tokens, tokens), 1)
    pick_keys = (placed == (stored & (ROWS - 1)) * STRIPES + (stored >> 7)).astype(F32).astype(BF)
    key_doc = lax.dot_general(
        by_pos, pick_keys, (((1,), (1,)), ((), ())), preferred_element_type=F32
    )[:1]
    mine = lax.broadcasted_iota(jnp.int32, (ROWS, tokens), 0) * STRIPES + s
    column = lax.broadcasted_iota(jnp.int32, (ROWS, tokens), 1)
    pick_rows = (column == mine).astype(F32).astype(BF)
    query_doc = lax.dot_general(
        pick_rows, by_pos, (((1,), (1,)), ((), ())), preferred_element_type=F32
    )[:, :1]
    key_pos = (column & (ROWS - 1)) * STRIPES + (column >> 7)
    allowed = (key_pos <= mine) & (key_doc == query_doc)
    bias[...] = jnp.where(allowed, 0.0, -1e30)

    sib_copy(1, 3).wait_recv()
    kv_arrival(0)
    early = [weigh(1, h) for h in range(2)]
    kv_arrival(1)
    for h in range(2):
        attend(1, h, early[h])
    for h in range(2):
        attend(2, h, weigh(2, h))

    pltpu.make_async_copy(part, part, send_sem).wait()


def fused(activations, query_weight, key_weight, value_weight, document_ids):
    depth = activations.shape[1]
    operands = (
        activations, document_ids.reshape(1, -1), query_weight, key_weight, value_weight,
    )
    return pl.pallas_call(
        fused_kernel,
        out_shape=jax.ShapeDtypeStruct((ROWS, 4 * HD), BF),
        in_specs=[pl.BlockSpec(memory_space=pltpu.HBM)] * 5,
        out_specs=pl.BlockSpec(memory_space=pltpu.VMEM),
        scratch_shapes=[
            pltpu.VMEM((ROWS, depth), BF),
            pltpu.VMEM((1, STRIPES * ROWS), jnp.int32),
            pltpu.VMEM((CHIPS, depth, 1024), BF),
            pltpu.VMEM((CHIPS, depth, 512), BF),
            pltpu.VMEM((2, PIECES, CHIPS, ROWS, WIDE), BF),
            pltpu.VMEM((PIECES, CHIPS, ROWS, WIDE), BF),
            pltpu.VMEM((PIECES, CHIPS, ROWS, WIDE), BF),
            pltpu.VMEM((2, STRIPES, ROWS, HD), BF),
            pltpu.VMEM((ROWS, STRIPES * ROWS), F32),
            pltpu.SemaphoreType.DMA((2,)),
            pltpu.SemaphoreType.DMA((2,)),
            pltpu.SemaphoreType.DMA((CHIPS,)),
            pltpu.SemaphoreType.DMA,
            pltpu.SemaphoreType.DMA((2, CHIPS)),
            pltpu.SemaphoreType.DMA((2,)),
            pltpu.SemaphoreType.DMA((19,)),
            pltpu.SemaphoreType.DMA((2,)),
            pltpu.SemaphoreType.REGULAR,
            pltpu.SemaphoreType.REGULAR,
            pltpu.SemaphoreType.REGULAR,
        ],
        compiler_params=pltpu.CompilerParams(
            collective_id=0, has_side_effects=True, vmem_limit_bytes=53 * 1024 * 1024
        ),
    )(*[pltpu.with_memory_space_constraint(operand, pltpu.HBM) for operand in operands])


def solution(mesh):
    small = mesh.shape["seq"] == STRIPES and mesh.shape["feat"] == 2 * CHIPS
    return jax.shard_map(
        fused if small else local,
        mesh=mesh,
        in_specs=(P("seq", "feat"), P("feat", None), P("feat", None), P("feat", None), P()),
        out_specs=P("seq", "feat"),
        check_vma=False,
    )
```
